32 devices in a mesh: band: 4 (over y, x), cell: 8 (over z, core).
Axes of the slice: x: 2, y: 2, z: 4, core: 2. Of those that a mesh axis runs over, the one named last changes fastest.
Arguments:
- wavefunctions: bfloat16 [512, 28672], P('band', 'cell'), may hold values from -24 to 24
- stiffness: bfloat16 [512, 512], replicated, may hold values from -1 to 2
- cell_scale: float32 [64], P('cell'), may hold values from 0.5 to 1.5
- potential: float32 [64, 512], P('cell'), may hold values from 0 to 1
Outputs:
- rotated: bfloat16 [512, 28672], P('band', 'cell')
The draws below stay inside these ranges and needn't reach their ends.
All inputs are finite; a program needn't handle non-finite values.
Results may differ from the reference program's by a relative error of at most 0.0022.
The reference program's roundings to bfloat16 on the way count: a program that leaves them out, or rounds other values in their place, can miss the bound.
Values may be sent and summed in bfloat16 or wider, within the bound.
A program may use at most 64 MiB of HBM per device.

```python
import math
from functools import partial
import jax
import jax.numpy as jnp
from jax import lax

NB = 512
CN = 512
PLANE = 64
OWN = 448
NCELLS = 64
NODES = 28672


def draw_wavefunctions(key, part):
    key_base, key_order, key_scale = jax.random.split(jax.random.fold_in(key, 11), 3)
    base = jnp.clip(jax.random.normal(key_base, (NB, NODES), jnp.float32), -5.0, 5.0)
    order = jax.random.permutation(key_order, NB)
    mixed = base + 0.6 * base[order]
    scales = jnp.exp(jax.random.uniform(key_scale, (NB, 1), jnp.float32, math.log(0.3), math.log(3.0)))
    return (mixed * scales).astype(jnp.bfloat16)


def draw_stiffness(key, part):
    key_noise, key_diag = jax.random.split(jax.random.fold_in(key, 23), 2)
    noise = jnp.clip(jax.random.normal(key_noise, (CN, CN), jnp.float32), -5.0, 5.0)
    diagonal = jax.random.uniform(key_diag, (CN,), jnp.float32, 1.0, 1.5)
    symmetric = (noise + noise.T) * (0.25 / math.sqrt(2.0 * CN))
    return (symmetric + jnp.diag(diagonal)).astype(jnp.bfloat16)


def shard_levels(own_key, extent, cuts, smallest, high):
    def one(dim, shards_of):
        steps = jax.random.uniform(jax.random.fold_in(jax.random.fold_in(own_key, 6), dim), (shards_of,), jnp.float32, smallest / len(cuts), high / len(cuts))
        return jnp.repeat(jnp.exp(steps), extent[dim] // shards_of).reshape((-1,) + (1,) * (len(extent) - dim - 1))

    loudness = one(*cuts[0])
    for cut in cuts[1:]:
        loudness = loudness * one(*cut)
    return loudness


def setup_inputs(seed: int = 0) -> dict:
    key_of = jax.random.split(jax.random.key(seed), 5)
    wavefunctions = draw_wavefunctions(jax.random.fold_in(key_of[4], 71), 0)
    stiffness = draw_stiffness(jax.random.fold_in(key_of[4], 71), 0)
    cell_scale = jnp.clip(jnp.exp(math.log(1.5) - 1.0986123 * jax.random.uniform(key_of[2], (NCELLS,), jnp.float32) ** shard_levels(key_of[2], (NCELLS,), ((0, 8),), -0.2, 0.2)), 0.5, 1.5)
    potential = jnp.clip(1.0 * jax.random.uniform(key_of[3], (NCELLS, CN), jnp.float32) ** shard_levels(key_of[3], (NCELLS, CN), ((0, 8),), -0.2, 0.2), 0.0, 1.0)
    return dict(wavefunctions=wavefunctions, stiffness=stiffness, cell_scale=cell_scale, potential=potential)


centre = 4.0
half_width = 3.0

def apply_group(group, stiffness, cell_scale, potential):
    band_rows = group.shape[0]
    owned_part = group.reshape(band_rows, NCELLS, OWN)
    top_plane = jnp.roll(owned_part, -1, axis=1)[:, :, :PLANE]
    cell_nodes = jnp.concatenate([owned_part, top_plane], 2).astype(jnp.float32)
    stiff_part = jnp.einsum('bcn,nm->bcm', cell_nodes, stiffness.astype(jnp.float32))
    cell_result = cell_scale[None, :, None] * stiff_part + potential[None] * cell_nodes
    spill = jnp.roll(cell_result[:, :, OWN:], 1, axis=1)
    kept = cell_result[:, :, :OWN]
    kept = jnp.concatenate([kept[:, :, :PLANE] + spill, kept[:, :, PLANE:]], 2)
    return kept.reshape(band_rows, NCELLS * OWN)

def apply_h(field, stiffness, cell_scale, potential):
    groups = field.reshape(-1, 64, field.shape[1])
    result = lax.map(partial(apply_group, stiffness=stiffness, cell_scale=cell_scale, potential=potential), groups)
    return result.reshape(field.shape[0], field.shape[1])

def reference(wavefunctions, stiffness, cell_scale, potential):
    anchor = wavefunctions.astype(jnp.float32)
    degree_one = ((apply_h(wavefunctions, stiffness, cell_scale, potential) - centre * anchor) / half_width).astype(jnp.bfloat16)
    one_wide = degree_one.astype(jnp.float32)
    degree_two = (2.0 * (apply_h(degree_one, stiffness, cell_scale, potential) - centre * one_wide) / half_width - anchor).astype(jnp.bfloat16)
    two_wide = degree_two.astype(jnp.float32)
    degree_three = (2.0 * (apply_h(degree_two, stiffness, cell_scale, potential) - centre * two_wide) / half_width - one_wide).astype(jnp.bfloat16)
    margin = jnp.dot(degree_three.astype(jnp.float32), degree_three.T.astype(jnp.float32), preferred_element_type=jnp.float32) / NODES
    factor = jnp.linalg.cholesky(margin)
    identity = jnp.eye(NB, dtype=jnp.float32)
    inverse = jax.scipy.linalg.solve_triangular(factor, identity, lower=True).astype(jnp.bfloat16)
    return jnp.dot(inverse.astype(jnp.float32), degree_three.astype(jnp.float32), preferred_element_type=jnp.float32).astype(jnp.bfloat16)
```

```python
import functools
import jax
import jax.numpy as jnp
from jax import lax
from jax.experimental import pallas as pl
from jax.experimental.pallas import tpu as pltpu
from jax.sharding import PartitionSpec as P

PLANE = 64
OWN = 448
BLK = 128
PAN = 8
MESH = pl.DeviceIdType.MESH

centre = 4.0
half_width = 3.0


def shifted(block, axis, distance):
    devices = range(lax.axis_size(axis))
    route = [((i - distance) % len(devices), i) for i in devices]
    return lax.ppermute(block, axis, route)


def apply_h(field, stiffness, cell_scale, potential):
    band_rows = field.shape[0]
    cell_count = field.shape[1] // OWN
    following = shifted(field[:, :PLANE], "cell", -1)
    owned_part = field.reshape(band_rows, cell_count, OWN)
    top_plane = jnp.concatenate([owned_part[:, 1:, :PLANE], following[:, None, :]], 1)
    cell_nodes = jnp.concatenate([owned_part, top_plane], 2)
    stiff_part = jnp.einsum(
        "bcn,nm->bcm", cell_nodes, stiffness, preferred_element_type=jnp.float32
    )
    cell_result = cell_scale[None, :, None] * stiff_part + potential[None] * cell_nodes.astype(
        jnp.float32
    )
    spill = cell_result[:, :, OWN:]
    incoming = shifted(spill[:, -1], "cell", 1)
    spill = jnp.concatenate([incoming[:, None, :], spill[:, :-1]], 1)
    kept = cell_result[:, :, :OWN]
    kept = jnp.concatenate([kept[:, :, :PLANE] + spill, kept[:, :, PLANE:]], 2)
    return kept.reshape(band_rows, cell_count * OWN)


def place(i, j, count):
    if i >= count // 2:
        return (count - 1 - i) * BLK, j * BLK
    return i * BLK, (count - i + j) * BLK


def packed_gram(slices_ref, packed_ref, count):
    for i in range(count):
        row, col = place(i, 0, count)
        width = (i + 1) * BLK
        packed_ref[row : row + BLK, col : col + width] = lax.dot_general(
            slices_ref[i * BLK : (i + 1) * BLK, :],
            slices_ref[:width, :],
            (((1,), (1,)), ((), ())),
            preferred_element_type=jnp.float32,
        )


def gram_kernel(count, slices_ref, packed_ref):
    packed_gram(slices_ref, packed_ref, count)


def reduce_kernel(
    count, bands, cells, total,
    slices_ref, out_ref,
    mine, from_core, half, from_band, quarter, from_z, piece,
    send_sem, recv_sem,
):
    band = lax.axis_index("band")
    cell = lax.axis_index("cell")
    core = lax.rem(cell, 2)
    level = lax.div(cell, 2)
    levels = cells // 2
    rows_half = mine.shape[0] // 2
    rows_band = rows_half // bands
    rows_z = rows_band // levels

    other_core = {"band": band, "cell": cell + 1 - 2 * core}
    band_peer = lambda o: lax.rem(band + o, bands)
    z_peer = lambda o: lax.rem(level + o, levels)
    band_device = lambda o: {"band": band_peer(o), "cell": cell}
    z_device = lambda o: {"band": band, "cell": z_peer(o) * 2 + core}

    barrier = pltpu.get_barrier_semaphore()
    pl.semaphore_signal(barrier, inc=1, device_id=other_core, device_id_type=MESH)
    for o in range(1, bands):
        pl.semaphore_signal(barrier, inc=1, device_id=band_device(o), device_id_type=MESH)
    for o in range(1, levels):
        pl.semaphore_signal(barrier, inc=1, device_id=z_device(o), device_id_type=MESH)

    packed_gram(slices_ref, mine, count)
    pl.semaphore_wait(barrier, 1 + (bands - 1) + (levels - 1))

    used = [0]

    def send(src, dst, device):
        slot = used[0]
        used[0] += 1
        copy = pltpu.make_async_remote_copy(
            src_ref=src, dst_ref=dst, send_sem=send_sem.at[slot], recv_sem=recv_sem.at[slot],
            device_id=device, device_id_type=MESH,
        )
        copy.start()
        return copy

    def rows(start, size):
        return pl.ds(pl.multiple_of(start, 8), size)

    copy = send(mine.at[rows((1 - core) * rows_half, rows_half)], from_core, other_core)
    copy.wait()
    half[...] = mine[rows(core * rows_half, rows_half), :] + from_core[...]

    copies = [
        send(half.at[rows(band_peer(o) * rows_band, rows_band)], from_band.at[o - 1], band_device(o))
        for o in range(1, bands)
    ]
    for copy in copies:
        copy.wait()
    summed = half[rows(band * rows_band, rows_band), :]
    for o in range(1, bands):
        summed = summed + from_band[o - 1]
    quarter[...] = summed

    copies = [
        send(quarter.at[rows(z_peer(o) * rows_z, rows_z)], from_z.at[o - 1], z_device(o))
        for o in range(1, levels)
    ]
    for copy in copies:
        copy.wait()
    summed = quarter[rows(level * rows_z, rows_z), :]
    for o in range(1, levels):
        summed = summed + from_z[o - 1]
    summed = summed / total
    piece[...] = summed

    start_half = core * rows_half
    start_band = start_half + band * rows_band
    start_z = start_band + level * rows_z
    here = rows(start_z, rows_z)
    out_ref[here, :] = summed
    copies = [send(piece, out_ref.at[here], z_device(o)) for o in range(1, levels)]
    for copy in copies:
        copy.wait()
    here = out_ref.at[rows(start_band, rows_band)]
    copies = [send(here, here, band_device(o)) for o in range(1, bands)]
    for copy in copies:
        copy.wait()
    here = out_ref.at[rows(start_half, rows_half)]
    send(here, here, other_core).wait()


def margin_packed(slices):
    bands, cells = lax.axis_size("band"), lax.axis_size("cell")
    band_total, nodes = slices.shape
    count = band_total // BLK
    total = float(nodes * bands * cells)
    height, width = band_total // 2, (count + 1) * BLK
    shape = jax.ShapeDtypeStruct((height, width), jnp.float32)
    vmem = pl.BlockSpec(memory_space=pltpu.VMEM)
    if cells % 2 or cells < 4 or bands < 2 or height % (8 * bands * cells):
        partial = pl.pallas_call(
            functools.partial(gram_kernel, count), out_shape=shape, in_specs=[vmem], out_specs=vmem
        )(slices)
        return lax.psum(partial, ("band", "cell")) / total
    levels = cells // 2
    rows_half = height // 2
    rows_band = rows_half // bands
    rows_z = rows_band // levels
    sends = 2 * (1 + (bands - 1) + (levels - 1))
    f32 = jnp.float32
    return pl.pallas_call(
        functools.partial(reduce_kernel, count, bands, cells, total),
        out_shape=shape,
        in_specs=[vmem],
        out_specs=vmem,
        scratch_shapes=[
            pltpu.VMEM((height, width), f32),
            pltpu.VMEM((rows_half, width), f32),
            pltpu.VMEM((rows_half, width), f32),
            pltpu.VMEM((bands - 1, rows_band, width), f32),
            pltpu.VMEM((rows_band, width), f32),
            pltpu.VMEM((levels - 1, rows_z, width), f32),
            pltpu.VMEM((rows_z, width), f32),
            pltpu.SemaphoreType.DMA((sends,)),
            pltpu.SemaphoreType.DMA((sends,)),
        ],
        compiler_params=pltpu.CompilerParams(collective_id=0, has_side_effects=True),
    )(slices)


def invert_block(block_ref):
    tiles = BLK // PAN
    shape = (PAN, BLK)
    lane = lax.broadcasted_iota(jnp.int32, shape, 1)
    row = lax.broadcasted_iota(jnp.int32, shape, 0)
    left = [block_ref[t * PAN : (t + 1) * PAN, :] for t in range(tiles)]
    right = [jnp.where(lane == row + t * PAN, 1.0, 0.0).astype(jnp.float32) for t in range(tiles)]

    def spread(value):
        return jnp.broadcast_to(value, shape)

    for m in range(tiles):
        k = m * PAN
        grid = {
            (i, j): spread(left[m][i : i + 1, k + j : k + j + 1])
            for j in range(PAN)
            for i in range(j, PAN)
        }
        cols = [
            [spread(left[t][:, k + j : k + j + 1]) for t in range(m + 1, tiles)] for j in range(PAN)
        ]
        rows_left = [spread(left[m][j : j + 1, :]) for j in range(PAN)]
        rows_right = [spread(right[m][j : j + 1, :]) for j in range(PAN)]
        for j in range(PAN):
            scale = lax.rsqrt(grid[j, j])
            rows_left[j] = rows_left[j] * scale
            rows_right[j] = rows_right[j] * scale
            cols[j] = [c * scale for c in cols[j]]
            factor = {i: grid[i, j] * scale for i in range(j + 1, PAN)}
            for i in range(j + 1, PAN):
                for q in range(j + 1, i + 1):
                    grid[i, q] = grid[i, q] - factor[i] * factor[q]
                rows_left[i] = rows_left[i] - factor[i] * rows_left[j]
                rows_right[i] = rows_right[i] - factor[i] * rows_right[j]
                cols[i] = [c - factor[i] * d for c, d in zip(cols[i], cols[j])]
        for n, t in enumerate(range(m + 1, tiles)):
            for j in range(PAN):
                left[t] = left[t] - cols[j][n] * rows_left[j]
                right[t] = right[t] - cols[j][n] * rows_right[j]
        done = rows_right[0]
        for j in range(1, PAN):
            done = jnp.where(row == j, rows_right[j], done)
        right[m] = done
    return right


def exact(a, b, dims):
    return lax.dot_general(
        a, b, (dims, ((), ())), precision=lax.Precision.HIGHEST, preferred_element_type=jnp.float32
    )


NN = ((1,), (0,))
NT = ((1,), (1,))


def factor_kernel(count, packed_ref, out_ref, work, lower, inv, diag):
    size = count * BLK
    for i in range(count):
        row, col = place(i, 0, count)
        width = (i + 1) * BLK
        work[i * BLK : (i + 1) * BLK, :width] = packed_ref[row : row + BLK, col : col + width]
    inv[...] = jnp.zeros_like(inv)
    diag[...] = work[:BLK, :BLK]

    @pl.loop(0, count)
    def _(step):
        tiles = invert_block(diag)
        for t, tile in enumerate(tiles):
            diag[t * PAN : (t + 1) * PAN, :] = tile
        for j in range(count):

            @pl.when(step == j)
            def _():
                here = slice(j * BLK, (j + 1) * BLK)
                top = diag[...]
                if j:
                    partial = exact(lower[here, : j * BLK], inv[: j * BLK, : j * BLK], NN)
                    inv[here, : j * BLK] = -exact(top, partial, NN)
                inv[here, here] = top
                if j + 1 < count:
                    below = slice((j + 1) * BLK, size)
                    panel = exact(work[below, here], top, NT)
                    lower[below, here] = panel
                    work[below, below] = work[below, below] - exact(panel, panel, NT)
                    diag[...] = work[(j + 1) * BLK : (j + 2) * BLK, (j + 1) * BLK : (j + 2) * BLK]

    out_ref[...] = inv[...].astype(out_ref.dtype)


def inverse_factor(packed):
    size = packed.shape[0] * 2
    count = size // BLK
    vmem = pl.BlockSpec(memory_space=pltpu.VMEM)
    return pl.pallas_call(
        functools.partial(factor_kernel, count),
        out_shape=jax.ShapeDtypeStruct((size, size), jnp.bfloat16),
        in_specs=[vmem],
        out_specs=vmem,
        scratch_shapes=[
            pltpu.VMEM((size, size), jnp.float32),
            pltpu.VMEM((size, size), jnp.float32),
            pltpu.VMEM((size, size), jnp.float32),
            pltpu.VMEM((BLK, BLK), jnp.float32),
        ],
    )(packed)


def shards(wavefunctions, stiffness, cell_scale, potential):
    anchor = wavefunctions.astype(jnp.float32)
    degree_one = (
        (apply_h(wavefunctions, stiffness, cell_scale, potential) - centre * anchor) / half_width
    ).astype(jnp.bfloat16)
    one_wide = degree_one.astype(jnp.float32)
    degree_two = (
        2.0
        * (apply_h(degree_one, stiffness, cell_scale, potential) - centre * one_wide)
        / half_width
        - anchor
    ).astype(jnp.bfloat16)
    two_wide = degree_two.astype(jnp.float32)
    degree_three = (
        2.0
        * (apply_h(degree_two, stiffness, cell_scale, potential) - centre * two_wide)
        / half_width
        - one_wide
    ).astype(jnp.bfloat16)
    slices = lax.all_to_all(degree_three, "band", split_axis=1, concat_axis=0, tiled=True)
    inverse = inverse_factor(margin_packed(slices))
    rotated = jnp.dot(inverse, slices, preferred_element_type=jnp.float32).astype(jnp.bfloat16)
    return lax.all_to_all(rotated, "band", split_axis=0, concat_axis=1, tiled=True)


def solution(mesh):
    in_specs = (P("band", "cell"), P(), P("cell"), P("cell", None))
    out_specs = P("band", "cell")
    return jax.shard_map(shards, mesh=mesh, in_specs=in_specs, out_specs=out_specs, check_vma=False)
```

```python
import functools
import jax
import jax.numpy as jnp
from jax import lax
from jax.experimental import pallas as pl
from jax.experimental.pallas import tpu as pltpu
from jax.sharding import PartitionSpec as P

PLANE = 64
OWN = 448
BLK = 128
PAN = 8
MESH = pl.DeviceIdType.MESH

centre = 4.0
half_width = 3.0


def shifted(block, axis, distance):
    devices = range(lax.axis_size(axis))
    route = [((i - distance) % len(devices), i) for i in devices]
    return lax.ppermute(block, axis, route)


def apply_h(field, stiffness, cell_scale, potential):
    band_rows = field.shape[0]
    cell_count = field.shape[1] // OWN
    following = shifted(field[:, :PLANE], "cell", -1)
    owned_part = field.reshape(band_rows, cell_count, OWN)
    top_plane = jnp.concatenate([owned_part[:, 1:, :PLANE], following[:, None, :]], 1)
    cell_nodes = jnp.concatenate([owned_part, top_plane], 2)
    stiff_part = jnp.einsum(
        "bcn,nm->bcm", cell_nodes, stiffness, preferred_element_type=jnp.float32
    )
    cell_result = cell_scale[None, :, None] * stiff_part + potential[None] * cell_nodes.astype(
        jnp.float32
    )
    spill = cell_result[:, :, OWN:]
    incoming = shifted(spill[:, -1], "cell", 1)
    spill = jnp.concatenate([incoming[:, None, :], spill[:, :-1]], 1)
    kept = cell_result[:, :, :OWN]
    kept = jnp.concatenate([kept[:, :, :PLANE] + spill, kept[:, :, PLANE:]], 2)
    return kept.reshape(band_rows, cell_count * OWN)


def place(i, j, count):
    if i >= count // 2:
        return (count - 1 - i) * BLK, j * BLK
    return i * BLK, (count - i + j) * BLK


def packed_gram(slices_ref, packed_ref, count):
    for i in range(count):
        row, col = place(i, 0, count)
        width = (i + 1) * BLK
        packed_ref[row : row + BLK, col : col + width] = lax.dot_general(
            slices_ref[i * BLK : (i + 1) * BLK, :],
            slices_ref[:width, :],
            (((1,), (1,)), ((), ())),
            preferred_element_type=jnp.float32,
        )


def gram_kernel(count, slices_ref, packed_ref):
    packed_gram(slices_ref, packed_ref, count)


def rows_at(start, size):
    return pl.ds(pl.multiple_of(start, 8), size)


def pair_step(e, degree, source, older, target, st, potb, potx):
    at = lambda c, skip, size: pl.ds(pl.multiple_of(c * OWN + skip, 16), size)
    nodes = OWN + PLANE
    va, vb = source[at(e, 0, nodes), :], source[at(e + 1, 0, nodes), :]
    vp = source[at(e - 1, 0, nodes), :]
    both = jnp.dot(st[...], jnp.concatenate([va, vb], 1), preferred_element_type=jnp.float32)
    before = jnp.dot(st[OWN:nodes, :], vp, preferred_element_type=jnp.float32)
    scale = lambda c: potx[c][:, nodes:]
    wa, wb = va.astype(jnp.float32), vb.astype(jnp.float32)
    ya = scale(e) * both[:, :BLK] + potb[e] * wa
    yb = scale(e + 1) * both[:, BLK:] + potb[e + 1] * wb
    yp = scale(e - 1) * before + potb[e - 1, OWN:, :] * vp[OWN:].astype(jnp.float32)

    def finish(c, h, w, skip):
        size = h.shape[0]
        value = h - centre * w
        if degree == 1:
            value = value * (1.0 / half_width)
        else:
            value = value * (2.0 / half_width) - older[at(c, skip, size), :].astype(jnp.float32)
        target[at(c, skip, size), :] = value.astype(target.dtype)

    finish(e, ya[:PLANE] + yp, wa[:PLANE], 0)
    finish(e, ya[PLANE:OWN], wa[PLANE:OWN], PLANE)
    finish(e + 1, yb[:PLANE] + ya[OWN:], wb[:PLANE], 0)
    finish(e + 1, yb[PLANE:OWN], wb[PLANE:OWN], PLANE)


def filter_kernel(
    count, bands, cells, held, total,
    wave_ref, stiff_ref, pots_ref, slices_ref, out_ref,
    ext, one, two, three, st, potx, potb,
    mine, from_core, half, from_band, quarter, from_z, piece,
    send_sem, recv_sem,
):
    band = lax.axis_index("band")
    cell = lax.axis_index("cell")
    core = lax.rem(cell, 2)
    level = lax.div(cell, 2)
    levels = cells // 2
    rows_half = mine.shape[0] // 2
    rows_band = rows_half // bands
    rows_z = rows_band // levels
    nodes = OWN + PLANE
    owned = held * OWN

    other_core = {"band": band, "cell": cell + 1 - 2 * core}
    band_peer = lambda o: lax.rem(band + o, bands)
    z_peer = lambda o: lax.rem(level + o, levels)
    band_device = lambda o: {"band": band_peer(o), "cell": cell}
    z_device = lambda o: {"band": band, "cell": z_peer(o) * 2 + core}
    cell_device = lambda o: {"band": band, "cell": lax.rem(cell + o, cells)}

    barrier = pltpu.get_barrier_semaphore()
    for o in range(1, bands):
        pl.semaphore_signal(barrier, inc=1, device_id=band_device(o), device_id_type=MESH)
    for o in range(1, cells):
        pl.semaphore_signal(barrier, inc=1, device_id=cell_device(o), device_id_type=MESH)
    pl.semaphore_wait(barrier, bands - 1 + cells - 1)

    used = [0]

    def send(src, dst, device):
        slot = used[0]
        used[0] += 1
        copy = pltpu.make_async_remote_copy(
            src_ref=src, dst_ref=dst, send_sem=send_sem.at[slot], recv_sem=recv_sem.at[slot],
            device_id=device, device_id_type=MESH,
        )
        copy.start()
        return copy

    low, high = 3 * OWN, 2 * OWN + PLANE
    right, left = cell_device(1), cell_device(cells - 1)
    halo = [
        send(pots_ref.at[held - 3 : held], potx.at[0:3], right),
        send(pots_ref.at[0:2], potx.at[held + 3 : held + 5], left),
        send(wave_ref.at[owned - low : owned], ext.at[0:low], right),
        send(wave_ref.at[0:high], ext.at[low + owned : low + owned + high], left),
    ]
    potx[3 : held + 3] = pots_ref[...]
    ext[low : low + owned, :] = wave_ref[...]
    st[...] = stiff_ref[...].T

    def columns(c):
        line = potx[c]
        for q in range(nodes // BLK):
            part = jnp.broadcast_to(line[:, q * BLK : (q + 1) * BLK], (BLK, BLK))
            potb[c, q * BLK : (q + 1) * BLK, :] = part.T

    @pl.loop(3, held + 3)
    def _(c):
        columns(c)

    @pl.loop(0, (held - 4) // 2)
    def _(p):
        pair_step(5 + 2 * p, 1, ext, None, one, st, potb, potx)

    for copy in halo:
        copy.wait()
    for c in (0, 1, 2, held + 3, held + 4):
        columns(c)

    @pl.loop(0, 4)
    def _(p):
        e = jnp.where(p < 2, 1 + 2 * p, held - 3 + 2 * p)
        pair_step(e, 1, ext, None, one, st, potb, potx)

    @pl.loop(0, held // 2 + 1)
    def _(p):
        pair_step(2 + 2 * p, 2, one, ext, two, st, potb, potx)

    each = owned // bands
    pairs = held // 2 // bands
    base = used[0]
    used[0] += bands - 1
    swaps = []
    for o in [*range(1, bands), 0]:
        peer = band_peer(o)

        @pl.loop(0, pairs)
        def _(p):
            pair_step(3 + 2 * (peer * pairs + p), 3, two, one, three, st, potb, potx)

        piece_of = three.at[pl.ds(pl.multiple_of(low + peer * each, 16), each)]
        if o:
            copy = pltpu.make_async_remote_copy(
                src_ref=piece_of, dst_ref=slices_ref.at[band],
                send_sem=send_sem.at[base + o - 1], recv_sem=recv_sem.at[base + o - 1],
                device_id=band_device(o), device_id_type=MESH,
            )
            copy.start()
            swaps.append(copy)
        else:
            slices_ref[band] = piece_of[...]
    for copy in swaps:
        copy.wait()

    for i in range(count):
        row, col = place(i, 0, count)
        width = (i + 1) * BLK
        joined = jnp.concatenate([slices_ref[j] for j in range(i + 1)], 1)
        mine[row : row + BLK, col : col + width] = jnp.dot(
            slices_ref[i].T, joined, preferred_element_type=jnp.float32
        )

    copy = send(mine.at[rows_at((1 - core) * rows_half, rows_half)], from_core, other_core)
    copy.wait()
    half[...] = mine[rows_at(core * rows_half, rows_half), :] + from_core[...]

    copies = [
        send(half.at[rows_at(band_peer(o) * rows_band, rows_band)], from_band.at[o - 1], band_device(o))
        for o in range(1, bands)
    ]
    for copy in copies:
        copy.wait()
    summed = half[rows_at(band * rows_band, rows_band), :]
    for o in range(1, bands):
        summed = summed + from_band[o - 1]
    quarter[...] = summed

    copies = [
        send(quarter.at[rows_at(z_peer(o) * rows_z, rows_z)], from_z.at[o - 1], z_device(o))
        for o in range(1, levels)
    ]
    for copy in copies:
        copy.wait()
    summed = quarter[rows_at(level * rows_z, rows_z), :]
    for o in range(1, levels):
        summed = summed + from_z[o - 1]
    summed = summed / total
    piece[...] = summed

    start_half = core * rows_half
    start_band = start_half + band * rows_band
    start_z = start_band + level * rows_z
    here = rows_at(start_z, rows_z)
    out_ref[here, :] = summed
    copies = [send(piece, out_ref.at[here], z_device(o)) for o in range(1, levels)]
    for copy in copies:
        copy.wait()
    here = out_ref.at[rows_at(start_band, rows_band)]
    copies = [send(here, here, band_device(o)) for o in range(1, bands)]
    for copy in copies:
        copy.wait()
    here = out_ref.at[rows_at(start_half, rows_half)]
    send(here, here, other_core).wait()


def filtered(wavefunctions, stiffness, cell_scale, potential):
    bands, cells = lax.axis_size("band"), lax.axis_size("cell")
    band_rows, owned = wavefunctions.shape
    held = owned // OWN
    nodes = OWN + PLANE
    count = band_rows * bands // BLK
    each = owned // bands
    total = float(owned * cells)
    height, width = count * BLK // 2, (count + 1) * BLK
    levels = cells // 2
    rows_half = height // 2
    rows_band = rows_half // bands
    rows_z = rows_band // levels
    sends = 4 + (bands - 1) + 2 * (1 + (bands - 1) + (levels - 1))
    spans = owned + 5 * OWN + PLANE
    scales = jnp.broadcast_to(cell_scale[:, None], (held, BLK))
    pots = jnp.concatenate([potential, scales], 1)[:, None, :]
    vmem = pl.BlockSpec(memory_space=pltpu.VMEM)
    f32, bf16 = jnp.float32, jnp.bfloat16
    return pl.pallas_call(
        functools.partial(filter_kernel, count, bands, cells, held, total),
        out_shape=(
            jax.ShapeDtypeStruct((bands, each, BLK), bf16),
            jax.ShapeDtypeStruct((height, width), f32),
        ),
        in_specs=[vmem] * 3,
        out_specs=(vmem, vmem),
        scratch_shapes=[
            pltpu.VMEM((spans, BLK), bf16),
            pltpu.VMEM((spans, BLK), bf16),
            pltpu.VMEM((spans, BLK), bf16),
            pltpu.VMEM((spans, BLK), bf16),
            pltpu.VMEM((nodes, nodes), bf16),
            pltpu.VMEM((held + 5, 1, nodes + BLK), f32),
            pltpu.VMEM((held + 5, nodes, BLK), f32),
            pltpu.VMEM((height, width), f32),
            pltpu.VMEM((rows_half, width), f32),
            pltpu.VMEM((rows_half, width), f32),
            pltpu.VMEM((bands - 1, rows_band, width), f32),
            pltpu.VMEM((rows_band, width), f32),
            pltpu.VMEM((levels - 1, rows_z, width), f32),
            pltpu.VMEM((rows_z, width), f32),
            pltpu.SemaphoreType.DMA((sends,)),
            pltpu.SemaphoreType.DMA((sends,)),
        ],
        compiler_params=pltpu.CompilerParams(collective_id=0, has_side_effects=True),
    )(wavefunctions.T, stiffness, pots)


def rotate_kernel(bands, inverse_ref, slices_ref, out_ref, rotated, send_sem, recv_sem):
    band = lax.axis_index("band")
    cell = lax.axis_index("cell")
    each = slices_ref.shape[1]
    peer = lambda o: lax.rem(band + o, bands)
    device = lambda o: {"band": peer(o), "cell": cell}
    barrier = pltpu.get_barrier_semaphore()
    for o in range(1, bands):
        pl.semaphore_signal(barrier, inc=1, device_id=device(o), device_id_type=MESH)
    pl.semaphore_wait(barrier, bands - 1)
    joined = jnp.concatenate([slices_ref[j] for j in range(bands)], 1)
    here = pl.ds(pl.multiple_of(band * each, BLK), each)
    copies = []
    for o in [*range(1, bands), 0]:
        some = inverse_ref[rows_at(peer(o) * BLK, BLK), :]
        value = lax.dot_general(
            some, joined, (((1,), (1,)), ((), ())), preferred_element_type=jnp.float32
        ).astype(out_ref.dtype)
        if o == 0:
            out_ref[:, here] = value
            continue
        rotated[o - 1] = value
        copy = pltpu.make_async_remote_copy(
            src_ref=rotated.at[o - 1], dst_ref=out_ref.at[:, here],
            send_sem=send_sem.at[o - 1], recv_sem=recv_sem.at[o - 1],
            device_id=device(o), device_id_type=MESH,
        )
        copy.start()
        copies.append(copy)
    for copy in copies:
        copy.wait()


def rotated_back(inverse, slices):
    bands, each, wide = slices.shape
    vmem = pl.BlockSpec(memory_space=pltpu.VMEM)
    return pl.pallas_call(
        functools.partial(rotate_kernel, bands),
        out_shape=jax.ShapeDtypeStruct((wide, bands * each), slices.dtype),
        in_specs=[vmem, vmem],
        out_specs=vmem,
        scratch_shapes=[
            pltpu.VMEM((bands - 1, wide, each), slices.dtype),
            pltpu.SemaphoreType.DMA((bands - 1,)),
            pltpu.SemaphoreType.DMA((bands - 1,)),
        ],
        compiler_params=pltpu.CompilerParams(collective_id=1, has_side_effects=True),
    )(inverse, slices)


def fits(band_rows, owned, bands, cells):
    height = band_rows * bands // 2
    return (
        band_rows == BLK
        and owned % OWN == 0
        and bands >= 2
        and cells % 2 == 0
        and cells >= 4
        and owned // OWN >= 4
        and owned // OWN % (2 * bands) == 0
        and height % (16 * bands * (cells // 2)) == 0
    )


def margin_packed(slices):
    bands, cells = lax.axis_size("band"), lax.axis_size("cell")
    band_total, nodes = slices.shape
    count = band_total // BLK
    shape = jax.ShapeDtypeStruct((band_total // 2, (count + 1) * BLK), jnp.float32)
    vmem = pl.BlockSpec(memory_space=pltpu.VMEM)
    partial = pl.pallas_call(
        functools.partial(gram_kernel, count), out_shape=shape, in_specs=[vmem], out_specs=vmem
    )(slices)
    return lax.psum(partial, ("band", "cell")) / float(nodes * bands * cells)


def invert_block(block_ref):
    tiles = BLK // PAN
    shape = (PAN, BLK)
    lane = lax.broadcasted_iota(jnp.int32, shape, 1)
    row = lax.broadcasted_iota(jnp.int32, shape, 0)
    left = [block_ref[t * PAN : (t + 1) * PAN, :] for t in range(tiles)]
    right = [jnp.where(lane == row + t * PAN, 1.0, 0.0).astype(jnp.float32) for t in range(tiles)]

    def spread(value):
        return jnp.broadcast_to(value, shape)

    for m in range(tiles):
        k = m * PAN
        grid = {
            (i, j): spread(left[m][i : i + 1, k + j : k + j + 1])
            for j in range(PAN)
            for i in range(j, PAN)
        }
        cols = [
            [spread(left[t][:, k + j : k + j + 1]) for t in range(m + 1, tiles)] for j in range(PAN)
        ]
        rows_left = [spread(left[m][j : j + 1, :]) for j in range(PAN)]
        rows_right = [spread(right[m][j : j + 1, :]) for j in range(PAN)]
        for j in range(PAN):
            scale = lax.rsqrt(grid[j, j])
            rows_left[j] = rows_left[j] * scale
            rows_right[j] = rows_right[j] * scale
            cols[j] = [c * scale for c in cols[j]]
            factor = {i: grid[i, j] * scale for i in range(j + 1, PAN)}
            for i in range(j + 1, PAN):
                for q in range(j + 1, i + 1):
                    grid[i, q] = grid[i, q] - factor[i] * factor[q]
                rows_left[i] = rows_left[i] - factor[i] * rows_left[j]
                rows_right[i] = rows_right[i] - factor[i] * rows_right[j]
                cols[i] = [c - factor[i] * d for c, d in zip(cols[i], cols[j])]
        for n, t in enumerate(range(m + 1, tiles)):
            for j in range(PAN):
                left[t] = left[t] - cols[j][n] * rows_left[j]
                right[t] = right[t] - cols[j][n] * rows_right[j]
        done = rows_right[0]
        for j in range(1, PAN):
            done = jnp.where(row == j, rows_right[j], done)
        right[m] = done
    return right


def exact(a, b, dims):
    return lax.dot_general(
        a, b, (dims, ((), ())), precision=lax.Precision.HIGHEST, preferred_element_type=jnp.float32
    )


NN = ((1,), (0,))
NT = ((1,), (1,))


def factor_kernel(count, packed_ref, out_ref, work, lower, inv, diag):
    size = count * BLK
    for i in range(count):
        row, col = place(i, 0, count)
        width = (i + 1) * BLK
        work[i * BLK : (i + 1) * BLK, :width] = packed_ref[row : row + BLK, col : col + width]
    inv[...] = jnp.zeros_like(inv)
    diag[...] = work[:BLK, :BLK]

    @pl.loop(0, count)
    def _(step):
        tiles = invert_block(diag)
        for t, tile in enumerate(tiles):
            diag[t * PAN : (t + 1) * PAN, :] = tile
        for j in range(count):

            @pl.when(step == j)
            def _():
                here = slice(j * BLK, (j + 1) * BLK)
                top = diag[...]
                if j:
                    partial = exact(lower[here, : j * BLK], inv[: j * BLK, : j * BLK], NN)
                    inv[here, : j * BLK] = -exact(top, partial, NN)
                inv[here, here] = top
                if j + 1 < count:
                    below = slice((j + 1) * BLK, size)
                    panel = exact(work[below, here], top, NT)
                    lower[below, here] = panel
                    work[below, below] = work[below, below] - exact(panel, panel, NT)
                    diag[...] = work[(j + 1) * BLK : (j + 2) * BLK, (j + 1) * BLK : (j + 2) * BLK]

    out_ref[...] = inv[...].astype(out_ref.dtype)


def inverse_factor(packed):
    size = packed.shape[0] * 2
    count = size // BLK
    vmem = pl.BlockSpec(memory_space=pltpu.VMEM)
    return pl.pallas_call(
        functools.partial(factor_kernel, count),
        out_shape=jax.ShapeDtypeStruct((size, size), jnp.bfloat16),
        in_specs=[vmem],
        out_specs=vmem,
        scratch_shapes=[
            pltpu.VMEM((size, size), jnp.float32),
            pltpu.VMEM((size, size), jnp.float32),
            pltpu.VMEM((size, size), jnp.float32),
            pltpu.VMEM((BLK, BLK), jnp.float32),
        ],
    )(packed)


def shards(wavefunctions, stiffness, cell_scale, potential):
    if fits(*wavefunctions.shape, lax.axis_size("band"), lax.axis_size("cell")):
        slices, packed = filtered(wavefunctions, stiffness, cell_scale, potential)
        return rotated_back(inverse_factor(packed), slices)
    anchor = wavefunctions.astype(jnp.float32)
    degree_one = (
        (apply_h(wavefunctions, stiffness, cell_scale, potential) - centre * anchor) / half_width
    ).astype(jnp.bfloat16)
    one_wide = degree_one.astype(jnp.float32)
    degree_two = (
        2.0
        * (apply_h(degree_one, stiffness, cell_scale, potential) - centre * one_wide)
        / half_width
        - anchor
    ).astype(jnp.bfloat16)
    two_wide = degree_two.astype(jnp.float32)
    degree_three = (
        2.0
        * (apply_h(degree_two, stiffness, cell_scale, potential) - centre * two_wide)
        / half_width
        - one_wide
    ).astype(jnp.bfloat16)
    slices = lax.all_to_all(degree_three, "band", split_axis=1, concat_axis=0, tiled=True)
    inverse = inverse_factor(margin_packed(slices))
    rotated = jnp.dot(inverse, slices, preferred_element_type=jnp.float32).astype(jnp.bfloat16)
    return lax.all_to_all(rotated, "band", split_axis=0, concat_axis=1, tiled=True)


def solution(mesh):
    in_specs = (P("band", "cell"), P(), P("cell"), P("cell", None))
    out_specs = P("band", "cell")
    return jax.shard_map(shards, mesh=mesh, in_specs=in_specs, out_specs=out_specs, check_vma=False)
```

```python
import functools
import jax
import jax.numpy as jnp
from jax import lax
from jax.experimental import pallas as pl
from jax.experimental.pallas import tpu as pltpu
from jax.sharding import PartitionSpec as P

PLANE = 64
OWN = 448
BLK = 128
PAN = 8
MESH = pl.DeviceIdType.MESH

centre = 4.0
half_width = 3.0


def shifted(block, axis, distance):
    devices = range(lax.axis_size(axis))
    route = [((i - distance) % len(devices), i) for i in devices]
    return lax.ppermute(block, axis, route)


def apply_h(field, stiffness, cell_scale, potential):
    band_rows = field.shape[0]
    cell_count = field.shape[1] // OWN
    following = shifted(field[:, :PLANE], "cell", -1)
    owned_part = field.reshape(band_rows, cell_count, OWN)
    top_plane = jnp.concatenate([owned_part[:, 1:, :PLANE], following[:, None, :]], 1)
    cell_nodes = jnp.concatenate([owned_part, top_plane], 2)
    stiff_part = jnp.einsum(
        "bcn,nm->bcm", cell_nodes, stiffness, preferred_element_type=jnp.float32
    )
    cell_result = cell_scale[None, :, None] * stiff_part + potential[None] * cell_nodes.astype(
        jnp.float32
    )
    spill = cell_result[:, :, OWN:]
    incoming = shifted(spill[:, -1], "cell", 1)
    spill = jnp.concatenate([incoming[:, None, :], spill[:, :-1]], 1)
    kept = cell_result[:, :, :OWN]
    kept = jnp.concatenate([kept[:, :, :PLANE] + spill, kept[:, :, PLANE:]], 2)
    return kept.reshape(band_rows, cell_count * OWN)


def place(i, j, count):
    if i >= count // 2:
        return (count - 1 - i) * BLK, j * BLK
    return i * BLK, (count - i + j) * BLK


def packed_gram(slices_ref, packed_ref, count):
    for i in range(count):
        row, col = place(i, 0, count)
        width = (i + 1) * BLK
        packed_ref[row : row + BLK, col : col + width] = lax.dot_general(
            slices_ref[i * BLK : (i + 1) * BLK, :],
            slices_ref[:width, :],
            (((1,), (1,)), ((), ())),
            preferred_element_type=jnp.float32,
        )


def gram_kernel(count, slices_ref, packed_ref):
    packed_gram(slices_ref, packed_ref, count)


def rows_at(start, size):
    return pl.ds(pl.multiple_of(start, 8), size)


def pair_step(e, degree, source, older, target, st, potb, potx):
    at = lambda c, skip, size: pl.ds(pl.multiple_of(c * OWN + skip, 16), size)
    nodes = OWN + PLANE
    va, vb = source[at(e, 0, nodes), :], source[at(e + 1, 0, nodes), :]
    vp = source[at(e - 1, 0, nodes), :]
    both = jnp.dot(st[...], jnp.concatenate([va, vb], 1), preferred_element_type=jnp.float32)
    before = jnp.dot(st[OWN:nodes, :], vp, preferred_element_type=jnp.float32)
    scale = lambda c: potx[c][:, nodes:]
    wa, wb = va.astype(jnp.float32), vb.astype(jnp.float32)
    ya = scale(e) * both[:, :BLK] + potb[e] * wa
    yb = scale(e + 1) * both[:, BLK:] + potb[e + 1] * wb
    yp = scale(e - 1) * before + potb[e - 1, OWN:, :] * vp[OWN:].astype(jnp.float32)

    def finish(c, h, w, skip):
        size = h.shape[0]
        value = h - centre * w
        if degree == 1:
            value = value * (1.0 / half_width)
        else:
            value = value * (2.0 / half_width) - older[at(c, skip, size), :].astype(jnp.float32)
        target[at(c, skip, size), :] = value.astype(target.dtype)

    finish(e, ya[:PLANE] + yp, wa[:PLANE], 0)
    finish(e, ya[PLANE:OWN], wa[PLANE:OWN], PLANE)
    finish(e + 1, yb[:PLANE] + ya[OWN:], wb[:PLANE], 0)
    finish(e + 1, yb[PLANE:OWN], wb[PLANE:OWN], PLANE)


def filter_kernel(
    count, bands, cells, held, total,
    wave_ref, stiff_ref, scale_ref, potential_ref, slices_ref, out_ref,
    pots, turned, ext, one, two, three, st, potx, potb,
    mine, from_core, half, from_band, quarter, from_z, piece,
    send_sem, recv_sem,
):
    band = lax.axis_index("band")
    cell = lax.axis_index("cell")
    core = lax.rem(cell, 2)
    level = lax.div(cell, 2)
    levels = cells // 2
    rows_half = mine.shape[0] // 2
    rows_band = rows_half // bands
    rows_z = rows_band // levels
    nodes = OWN + PLANE
    owned = held * OWN

    other_core = {"band": band, "cell": cell + 1 - 2 * core}
    band_peer = lambda o: lax.rem(band + o, bands)
    z_peer = lambda o: lax.rem(level + o, levels)
    band_device = lambda o: {"band": band_peer(o), "cell": cell}
    z_device = lambda o: {"band": band, "cell": z_peer(o) * 2 + core}
    cell_device = lambda o: {"band": band, "cell": lax.rem(cell + o, cells)}

    barrier = pltpu.get_barrier_semaphore()
    for o in range(1, bands):
        pl.semaphore_signal(barrier, inc=1, device_id=band_device(o), device_id_type=MESH)
    for o in range(1, cells):
        pl.semaphore_signal(barrier, inc=1, device_id=cell_device(o), device_id_type=MESH)
    used = [0]

    def send(src, dst, device):
        slot = used[0]
        used[0] += 1
        copy = pltpu.make_async_remote_copy(
            src_ref=src, dst_ref=dst, send_sem=send_sem.at[slot], recv_sem=recv_sem.at[slot],
            device_id=device, device_id_type=MESH,
        )
        copy.start()
        return copy

    low, high = 3 * OWN, 2 * OWN + PLANE
    right, left = cell_device(1), cell_device(cells - 1)

    def turn(q):
        span = slice(q * BLK, (q + 1) * BLK)
        turned[span, :] = wave_ref[:, span].T

    strips = owned // BLK
    first, last = -(-high // BLK), (owned - low) // BLK
    for c in range(held):
        pots[c, :, :nodes] = potential_ref[c : c + 1, :]
        pots[c, :, nodes:] = jnp.broadcast_to(scale_ref[:, c : c + 1], (1, BLK))
    for q in range(last, strips):
        turn(q)
    pl.semaphore_wait(barrier, bands - 1 + cells - 1)
    halo = [
        send(pots.at[held - 3 : held], potx.at[0:3], right),
        send(pots.at[0:2], potx.at[held + 3 : held + 5], left),
        send(turned.at[owned - low : owned], ext.at[0:low], right),
    ]
    for q in range(first):
        turn(q)
    halo.append(send(turned.at[0:high], ext.at[low + owned : low + owned + high], left))
    for q in range(first, last):
        turn(q)
    potx[3 : held + 3] = pots[...]
    ext[low : low + owned, :] = turned[...]
    st[...] = stiff_ref[...].T

    def columns(c):
        line = potx[c]
        for q in range(nodes // BLK):
            part = jnp.broadcast_to(line[:, q * BLK : (q + 1) * BLK], (BLK, BLK))
            potb[c, q * BLK : (q + 1) * BLK, :] = part.T

    @pl.loop(3, held + 3)
    def _(c):
        columns(c)

    @pl.loop(0, (held - 4) // 2)
    def _(p):
        pair_step(5 + 2 * p, 1, ext, None, one, st, potb, potx)

    for copy in halo:
        copy.wait()
    for c in (0, 1, 2, held + 3, held + 4):
        columns(c)

    @pl.loop(0, 4)
    def _(p):
        e = jnp.where(p < 2, 1 + 2 * p, held - 3 + 2 * p)
        pair_step(e, 1, ext, None, one, st, potb, potx)

    @pl.loop(0, held // 2 + 1)
    def _(p):
        pair_step(2 + 2 * p, 2, one, ext, two, st, potb, potx)

    each = owned // bands
    pairs = held // 2 // bands
    base = used[0]
    used[0] += bands - 1
    swaps = []
    for o in [*range(1, bands), 0]:
        peer = band_peer(o)

        @pl.loop(0, pairs)
        def _(p):
            pair_step(3 + 2 * (peer * pairs + p), 3, two, one, three, st, potb, potx)

        piece_of = three.at[pl.ds(pl.multiple_of(low + peer * each, 16), each)]
        if o:
            copy = pltpu.make_async_remote_copy(
                src_ref=piece_of, dst_ref=slices_ref.at[band],
                send_sem=send_sem.at[base + o - 1], recv_sem=recv_sem.at[base + o - 1],
                device_id=band_device(o), device_id_type=MESH,
            )
            copy.start()
            swaps.append(copy)
        else:
            slices_ref[band] = piece_of[...]
    for copy in swaps:
        copy.wait()

    for i in range(count):
        row, col = place(i, 0, count)
        width = (i + 1) * BLK
        joined = jnp.concatenate([slices_ref[j] for j in range(i + 1)], 1)
        mine[row : row + BLK, col : col + width] = jnp.dot(
            slices_ref[i].T, joined, preferred_element_type=jnp.float32
        )

    copy = send(mine.at[rows_at((1 - core) * rows_half, rows_half)], from_core, other_core)
    copy.wait()
    half[...] = mine[rows_at(core * rows_half, rows_half), :] + from_core[...]

    copies = [
        send(half.at[rows_at(band_peer(o) * rows_band, rows_band)], from_band.at[o - 1], band_device(o))
        for o in range(1, bands)
    ]
    for copy in copies:
        copy.wait()
    summed = half[rows_at(band * rows_band, rows_band), :]
    for o in range(1, bands):
        summed = summed + from_band[o - 1]
    quarter[...] = summed

    copies = [
        send(quarter.at[rows_at(z_peer(o) * rows_z, rows_z)], from_z.at[o - 1], z_device(o))
        for o in range(1, levels)
    ]
    for copy in copies:
        copy.wait()
    summed = quarter[rows_at(level * rows_z, rows_z), :]
    for o in range(1, levels):
        summed = summed + from_z[o - 1]
    summed = summed / total
    piece[...] = summed

    start_half = core * rows_half
    start_band = start_half + band * rows_band
    start_z = start_band + level * rows_z
    here = rows_at(start_z, rows_z)
    out_ref[here, :] = summed
    copies = [send(piece, out_ref.at[here], z_device(o)) for o in range(1, levels)]
    for copy in copies:
        copy.wait()
    here = out_ref.at[rows_at(start_band, rows_band)]
    copies = [send(here, here, band_device(o)) for o in range(1, bands)]
    for copy in copies:
        copy.wait()
    here = out_ref.at[rows_at(start_half, rows_half)]
    send(here, here, other_core).wait()


def filtered(wavefunctions, stiffness, cell_scale, potential):
    bands, cells = lax.axis_size("band"), lax.axis_size("cell")
    band_rows, owned = wavefunctions.shape
    held = owned // OWN
    nodes = OWN + PLANE
    count = band_rows * bands // BLK
    each = owned // bands
    total = float(owned * cells)
    height, width = count * BLK // 2, (count + 1) * BLK
    levels = cells // 2
    rows_half = height // 2
    rows_band = rows_half // bands
    rows_z = rows_band // levels
    sends = 4 + (bands - 1) + 2 * (1 + (bands - 1) + (levels - 1))
    spans = owned + 5 * OWN + PLANE
    vmem = pl.BlockSpec(memory_space=pltpu.VMEM)
    f32, bf16 = jnp.float32, jnp.bfloat16
    return pl.pallas_call(
        functools.partial(filter_kernel, count, bands, cells, held, total),
        out_shape=(
            jax.ShapeDtypeStruct((bands, each, BLK), bf16),
            jax.ShapeDtypeStruct((height, width), f32),
        ),
        in_specs=[vmem] * 4,
        out_specs=(vmem, vmem),
        scratch_shapes=[
            pltpu.VMEM((held, 1, nodes + BLK), f32),
            pltpu.VMEM((owned, BLK), bf16),
            pltpu.VMEM((spans, BLK), bf16),
            pltpu.VMEM((spans, BLK), bf16),
            pltpu.VMEM((spans, BLK), bf16),
            pltpu.VMEM((spans, BLK), bf16),
            pltpu.VMEM((nodes, nodes), bf16),
            pltpu.VMEM((held + 5, 1, nodes + BLK), f32),
            pltpu.VMEM((held + 5, nodes, BLK), f32),
            pltpu.VMEM((height, width), f32),
            pltpu.VMEM((rows_half, width), f32),
            pltpu.VMEM((rows_half, width), f32),
            pltpu.VMEM((bands - 1, rows_band, width), f32),
            pltpu.VMEM((rows_band, width), f32),
            pltpu.VMEM((levels - 1, rows_z, width), f32),
            pltpu.VMEM((rows_z, width), f32),
            pltpu.SemaphoreType.DMA((sends,)),
            pltpu.SemaphoreType.DMA((sends,)),
        ],
        compiler_params=pltpu.CompilerParams(collective_id=0, has_side_effects=True),
    )(wavefunctions, stiffness, cell_scale[None, :], potential)


def rotate_kernel(bands, inverse_ref, slices_ref, out_ref, rotated, send_sem, recv_sem):
    band = lax.axis_index("band")
    cell = lax.axis_index("cell")
    each = slices_ref.shape[1]
    peer = lambda o: lax.rem(band + o, bands)
    device = lambda o: {"band": peer(o), "cell": cell}
    barrier = pltpu.get_barrier_semaphore()
    for o in range(1, bands):
        pl.semaphore_signal(barrier, inc=1, device_id=device(o), device_id_type=MESH)
    pl.semaphore_wait(barrier, bands - 1)
    joined = jnp.concatenate([slices_ref[j] for j in range(bands)], 1)
    here = pl.ds(pl.multiple_of(band * each, BLK), each)
    copies = []
    for o in [*range(1, bands), 0]:
        some = inverse_ref[rows_at(peer(o) * BLK, BLK), :]
        value = lax.dot_general(
            some, joined, (((1,), (1,)), ((), ())), preferred_element_type=jnp.float32
        ).astype(out_ref.dtype)
        if o == 0:
            out_ref[:, here] = value
            continue
        rotated[o - 1] = value
        copy = pltpu.make_async_remote_copy(
            src_ref=rotated.at[o - 1], dst_ref=out_ref.at[:, here],
            send_sem=send_sem.at[o - 1], recv_sem=recv_sem.at[o - 1],
            device_id=device(o), device_id_type=MESH,
        )
        copy.start()
        copies.append(copy)
    for copy in copies:
        copy.wait()


def rotated_back(inverse, slices):
    bands, each, wide = slices.shape
    vmem = pl.BlockSpec(memory_space=pltpu.VMEM)
    return pl.pallas_call(
        functools.partial(rotate_kernel, bands),
        out_shape=jax.ShapeDtypeStruct((wide, bands * each), slices.dtype),
        in_specs=[vmem, vmem],
        out_specs=vmem,
        scratch_shapes=[
            pltpu.VMEM((bands - 1, wide, each), slices.dtype),
            pltpu.SemaphoreType.DMA((bands - 1,)),
            pltpu.SemaphoreType.DMA((bands - 1,)),
        ],
        compiler_params=pltpu.CompilerParams(collective_id=1, has_side_effects=True),
    )(inverse, slices)


def fits(band_rows, owned, bands, cells):
    height = band_rows * bands // 2
    return (
        band_rows == BLK
        and owned % OWN == 0
        and bands >= 2
        and cells % 2 == 0
        and cells >= 4
        and owned // OWN >= 4
        and owned // OWN % (2 * bands) == 0
        and height % (16 * bands * (cells // 2)) == 0
    )


def margin_packed(slices):
    bands, cells = lax.axis_size("band"), lax.axis_size("cell")
    band_total, nodes = slices.shape
    count = band_total // BLK
    shape = jax.ShapeDtypeStruct((band_total // 2, (count + 1) * BLK), jnp.float32)
    vmem = pl.BlockSpec(memory_space=pltpu.VMEM)
    partial = pl.pallas_call(
        functools.partial(gram_kernel, count), out_shape=shape, in_specs=[vmem], out_specs=vmem
    )(slices)
    return lax.psum(partial, ("band", "cell")) / float(nodes * bands * cells)


def invert_block(block_ref):
    tiles = BLK // PAN
    shape = (PAN, BLK)
    lane = lax.broadcasted_iota(jnp.int32, shape, 1)
    row = lax.broadcasted_iota(jnp.int32, shape, 0)
    left = [block_ref[t * PAN : (t + 1) * PAN, :] for t in range(tiles)]
    right = [jnp.where(lane == row + t * PAN, 1.0, 0.0).astype(jnp.float32) for t in range(tiles)]

    def spread(value):
        return jnp.broadcast_to(value, shape)

    for m in range(tiles):
        k = m * PAN
        grid = {
            (i, j): spread(left[m][i : i + 1, k + j : k + j + 1])
            for j in range(PAN)
            for i in range(j, PAN)
        }
        cols = [
            [spread(left[t][:, k + j : k + j + 1]) for t in range(m + 1, tiles)] for j in range(PAN)
        ]
        rows_left = [spread(left[m][j : j + 1, :]) for j in range(PAN)]
        rows_right = [spread(right[m][j : j + 1, :]) for j in range(PAN)]
        for j in range(PAN):
            scale = lax.rsqrt(grid[j, j])
            rows_left[j] = rows_left[j] * scale
            rows_right[j] = rows_right[j] * scale
            cols[j] = [c * scale for c in cols[j]]
            factor = {i: grid[i, j] * scale for i in range(j + 1, PAN)}
            for i in range(j + 1, PAN):
                for q in range(j + 1, i + 1):
                    grid[i, q] = grid[i, q] - factor[i] * factor[q]
                rows_left[i] = rows_left[i] - factor[i] * rows_left[j]
                rows_right[i] = rows_right[i] - factor[i] * rows_right[j]
                cols[i] = [c - factor[i] * d for c, d in zip(cols[i], cols[j])]
        for n, t in enumerate(range(m + 1, tiles)):
            for j in range(PAN):
                left[t] = left[t] - cols[j][n] * rows_left[j]
                right[t] = right[t] - cols[j][n] * rows_right[j]
        done = rows_right[0]
        for j in range(1, PAN):
            done = jnp.where(row == j, rows_right[j], done)
        right[m] = done
    return right


def exact(a, b, dims):
    return lax.dot_general(
        a, b, (dims, ((), ())), precision=lax.Precision.HIGHEST, preferred_element_type=jnp.float32
    )


NN = ((1,), (0,))
NT = ((1,), (1,))


def factor_kernel(count, packed_ref, out_ref, work, lower, inv, diag):
    size = count * BLK
    for i in range(count):
        row, col = place(i, 0, count)
        width = (i + 1) * BLK
        work[i * BLK : (i + 1) * BLK, :width] = packed_ref[row : row + BLK, col : col + width]
    inv[...] = jnp.zeros_like(inv)
    diag[...] = work[:BLK, :BLK]

    @pl.loop(0, count)
    def _(step):
        tiles = invert_block(diag)
        for t, tile in enumerate(tiles):
            diag[t * PAN : (t + 1) * PAN, :] = tile
        for j in range(count):

            @pl.when(step == j)
            def _():
                here = slice(j * BLK, (j + 1) * BLK)
                top = diag[...]
                if j:
                    partial = exact(lower[here, : j * BLK], inv[: j * BLK, : j * BLK], NN)
                    inv[here, : j * BLK] = -exact(top, partial, NN)
                inv[here, here] = top
                if j + 1 < count:
                    below = slice((j + 1) * BLK, size)
                    panel = exact(work[below, here], top, NT)
                    lower[below, here] = panel
                    work[below, below] = work[below, below] - exact(panel, panel, NT)
                    diag[...] = work[(j + 1) * BLK : (j + 2) * BLK, (j + 1) * BLK : (j + 2) * BLK]

    out_ref[...] = inv[...].astype(out_ref.dtype)


def inverse_factor(packed):
    size = packed.shape[0] * 2
    count = size // BLK
    vmem = pl.BlockSpec(memory_space=pltpu.VMEM)
    return pl.pallas_call(
        functools.partial(factor_kernel, count),
        out_shape=jax.ShapeDtypeStruct((size, size), jnp.bfloat16),
        in_specs=[vmem],
        out_specs=vmem,
        scratch_shapes=[
            pltpu.VMEM((size, size), jnp.float32),
            pltpu.VMEM((size, size), jnp.float32),
            pltpu.VMEM((size, size), jnp.float32),
            pltpu.VMEM((BLK, BLK), jnp.float32),
        ],
    )(packed)


def shards(wavefunctions, stiffness, cell_scale, potential):
    if fits(*wavefunctions.shape, lax.axis_size("band"), lax.axis_size("cell")):
        slices, packed = filtered(wavefunctions, stiffness, cell_scale, potential)
        return rotated_back(inverse_factor(packed), slices)
    anchor = wavefunctions.astype(jnp.float32)
    degree_one = (
        (apply_h(wavefunctions, stiffness, cell_scale, potential) - centre * anchor) / half_width
    ).astype(jnp.bfloat16)
    one_wide = degree_one.astype(jnp.float32)
    degree_two = (
        2.0
        * (apply_h(degree_one, stiffness, cell_scale, potential) - centre * one_wide)
        / half_width
        - anchor
    ).astype(jnp.bfloat16)
    two_wide = degree_two.astype(jnp.float32)
    degree_three = (
        2.0
        * (apply_h(degree_two, stiffness, cell_scale, potential) - centre * two_wide)
        / half_width
        - one_wide
    ).astype(jnp.bfloat16)
    slices = lax.all_to_all(degree_three, "band", split_axis=1, concat_axis=0, tiled=True)
    inverse = inverse_factor(margin_packed(slices))
    rotated = jnp.dot(inverse, slices, preferred_element_type=jnp.float32).astype(jnp.bfloat16)
    return lax.all_to_all(rotated, "band", split_axis=0, concat_axis=1, tiled=True)


def solution(mesh):
    in_specs = (P("band", "cell"), P(), P("cell"), P("cell", None))
    out_specs = P("band", "cell")
    return jax.shard_map(shards, mesh=mesh, in_specs=in_specs, out_specs=out_specs, check_vma=False)
```

```python
import functools
import jax
import jax.numpy as jnp
from jax import lax
from jax.experimental import pallas as pl
from jax.experimental.pallas import tpu as pltpu
from jax.sharding import PartitionSpec as P

PLANE = 64
OWN = 448
BLK = 128
PAN = 8
MESH = pl.DeviceIdType.MESH

centre = 4.0
half_width = 3.0


def shifted(block, axis, distance):
    devices = range(lax.axis_size(axis))
    route = [((i - distance) % len(devices), i) for i in devices]
    return lax.ppermute(block, axis, route)


def apply_h(field, stiffness, cell_scale, potential):
    band_rows = field.shape[0]
    cell_count = field.shape[1] // OWN
    following = shifted(field[:, :PLANE], "cell", -1)
    owned_part = field.reshape(band_rows, cell_count, OWN)
    top_plane = jnp.concatenate([owned_part[:, 1:, :PLANE], following[:, None, :]], 1)
    cell_nodes = jnp.concatenate([owned_part, top_plane], 2)
    stiff_part = jnp.einsum(
        "bcn,nm->bcm", cell_nodes, stiffness, preferred_element_type=jnp.float32
    )
    cell_result = cell_scale[None, :, None] * stiff_part + potential[None] * cell_nodes.astype(
        jnp.float32
    )
    spill = cell_result[:, :, OWN:]
    incoming = shifted(spill[:, -1], "cell", 1)
    spill = jnp.concatenate([incoming[:, None, :], spill[:, :-1]], 1)
    kept = cell_result[:, :, :OWN]
    kept = jnp.concatenate([kept[:, :, :PLANE] + spill, kept[:, :, PLANE:]], 2)
    return kept.reshape(band_rows, cell_count * OWN)


def place(i, j, count):
    if i >= count // 2:
        return (count - 1 - i) * BLK, j * BLK
    return i * BLK, (count - i + j) * BLK


def packed_gram(slices_ref, packed_ref, count):
    for i in range(count):
        row, col = place(i, 0, count)
        width = (i + 1) * BLK
        packed_ref[row : row + BLK, col : col + width] = lax.dot_general(
            slices_ref[i * BLK : (i + 1) * BLK, :],
            slices_ref[:width, :],
            (((1,), (1,)), ((), ())),
            preferred_element_type=jnp.float32,
        )


def gram_kernel(count, slices_ref, packed_ref):
    packed_gram(slices_ref, packed_ref, count)


def rows_at(start, size):
    return pl.ds(pl.multiple_of(start, 8), size)


def pair_step(e, degree, source, older, target, st, potb, potx, shift=0):
    at = lambda c, skip, size: pl.ds(pl.multiple_of(c * OWN + skip, 16), size)
    nodes = OWN + PLANE
    va, vb = source[at(e, 0, nodes), :], source[at(e + 1, 0, nodes), :]
    vp = source[at(e - 1, 0, nodes), :]
    both = jnp.dot(st[...], jnp.concatenate([va, vb], 1), preferred_element_type=jnp.float32)
    before = jnp.dot(st[OWN:nodes, :], vp, preferred_element_type=jnp.float32)
    scale = lambda c: potx[c][:, nodes:]
    wa, wb = va.astype(jnp.float32), vb.astype(jnp.float32)
    ya = scale(e) * both[:, :BLK] + potb[e] * wa
    yb = scale(e + 1) * both[:, BLK:] + potb[e + 1] * wb
    yp = scale(e - 1) * before + potb[e - 1, OWN:, :] * vp[OWN:].astype(jnp.float32)

    def finish(c, h, w, skip):
        size = h.shape[0]
        value = h - centre * w
        if degree == 1:
            value = value * (1.0 / half_width)
        else:
            value = value * (2.0 / half_width) - older[at(c, skip, size), :].astype(jnp.float32)
        target[at(c - shift, skip, size), :] = value.astype(target.dtype)

    finish(e, ya[:PLANE] + yp, wa[:PLANE], 0)
    finish(e, ya[PLANE:OWN], wa[PLANE:OWN], PLANE)
    finish(e + 1, yb[:PLANE] + ya[OWN:], wb[:PLANE], 0)
    finish(e + 1, yb[PLANE:OWN], wb[PLANE:OWN], PLANE)


def send_ahead(turns, bands, band, cell, own_ref, ahead_ref, send_sem, recv_sem, base):
    each = ahead_ref.shape[2]
    wide = len(turns)
    device = lambda b: {"band": b, "cell": cell}

    def copy_to(b, n):
        part = (b + 1 + turns[n]) % bands
        return pltpu.make_async_remote_copy(
            src_ref=own_ref.at[part * each : (part + 1) * each], dst_ref=ahead_ref.at[band, n],
            send_sem=send_sem.at[base + (b - 1) * wide + n], recv_sem=recv_sem.at[base + band * wide + n],
            device_id=device(b), device_id_type=MESH,
        )

    def copy_from(h, n):
        return pltpu.make_async_remote_copy(
            src_ref=own_ref.at[0:each], dst_ref=ahead_ref.at[h, n],
            send_sem=send_sem.at[base + n], recv_sem=recv_sem.at[base + h * wide + n],
            device_id=device(h), device_id_type=MESH,
        )

    for n in range(wide):
        for b in range(1, bands):

            @pl.when(band < b)
            def _():
                copy_to(b, n).start()

    def finish():
        for n in range(wide):
            for b in range(1, bands):

                @pl.when(band < b)
                def _():
                    copy_to(b, n).wait_send()

                @pl.when(b - 1 < band)
                def _():
                    copy_from(b - 1, n).wait_recv()

    return finish


def filter_kernel(
    count, bands, cells, held, total,
    wave_ref, stiff_ref, scale_ref, potential_ref, slices_ref, three, ahead_ref, out_ref,
    pots, turned, ext, one, two, st, potx, potb,
    mine, from_core, half, from_band, quarter, from_z, piece,
    send_sem, recv_sem,
):
    band = lax.axis_index("band")
    cell = lax.axis_index("cell")
    core = lax.rem(cell, 2)
    level = lax.div(cell, 2)
    levels = cells // 2
    rows_half = mine.shape[0] // 2
    rows_band = rows_half // bands
    rows_z = rows_band // levels
    nodes = OWN + PLANE
    owned = held * OWN

    other_core = {"band": band, "cell": cell + 1 - 2 * core}
    band_peer = lambda o: lax.rem(band + o, bands)
    z_peer = lambda o: lax.rem(level + o, levels)
    band_device = lambda o: {"band": band_peer(o), "cell": cell}
    z_device = lambda o: {"band": band, "cell": z_peer(o) * 2 + core}
    cell_device = lambda o: {"band": band, "cell": lax.rem(cell + o, cells)}

    barrier = pltpu.get_barrier_semaphore()
    for o in range(1, bands):
        pl.semaphore_signal(barrier, inc=1, device_id=band_device(o), device_id_type=MESH)
    for o in range(1, cells):
        pl.semaphore_signal(barrier, inc=1, device_id=cell_device(o), device_id_type=MESH)
    used = [0]

    def send(src, dst, device):
        slot = used[0]
        used[0] += 1
        copy = pltpu.make_async_remote_copy(
            src_ref=src, dst_ref=dst, send_sem=send_sem.at[slot], recv_sem=recv_sem.at[slot],
            device_id=device, device_id_type=MESH,
        )
        copy.start()
        return copy

    low, high = 3 * OWN, 2 * OWN + PLANE
    right, left = cell_device(1), cell_device(cells - 1)

    def turn(q):
        span = slice(q * BLK, (q + 1) * BLK)
        turned[span, :] = wave_ref[:, span].T

    strips = owned // BLK
    first, last = -(-high // BLK), (owned - low) // BLK
    for c in range(held):
        pots[c, :, :nodes] = potential_ref[c : c + 1, :]
        pots[c, :, nodes:] = jnp.broadcast_to(scale_ref[:, c : c + 1], (1, BLK))
    for q in range(last, strips):
        turn(q)
    pl.semaphore_wait(barrier, bands - 1 + cells - 1)
    halo = [
        send(pots.at[held - 3 : held], potx.at[0:3], right),
        send(pots.at[0:2], potx.at[held + 3 : held + 5], left),
        send(turned.at[owned - low : owned], ext.at[0:low], right),
    ]
    for q in range(first):
        turn(q)
    halo.append(send(turned.at[0:high], ext.at[low + owned : low + owned + high], left))
    for q in range(first, last):
        turn(q)
    potx[3 : held + 3] = pots[...]
    ext[low : low + owned, :] = turned[...]
    st[...] = stiff_ref[...].T

    def columns(c):
        line = potx[c]
        for q in range(nodes // BLK):
            part = jnp.broadcast_to(line[:, q * BLK : (q + 1) * BLK], (BLK, BLK))
            potb[c, q * BLK : (q + 1) * BLK, :] = part.T

    @pl.loop(3, held + 3)
    def _(c):
        columns(c)

    @pl.loop(0, (held - 4) // 2)
    def _(p):
        pair_step(5 + 2 * p, 1, ext, None, one, st, potb, potx)

    for copy in halo:
        copy.wait()
    for c in (0, 1, 2, held + 3, held + 4):
        columns(c)

    @pl.loop(0, 4)
    def _(p):
        e = jnp.where(p < 2, 1 + 2 * p, held - 3 + 2 * p)
        pair_step(e, 1, ext, None, one, st, potb, potx)

    @pl.loop(0, held // 2 + 1)
    def _(p):
        pair_step(2 + 2 * p, 2, one, ext, two, st, potb, potx)

    each = owned // bands
    pairs = held // 2 // bands
    base = used[0]
    used[0] += bands - 1
    swaps = []
    for o in [*range(1, bands), 0]:
        peer = band_peer(o)

        @pl.loop(0, pairs)
        def _(p):
            pair_step(3 + 2 * (peer * pairs + p), 3, two, one, three, st, potb, potx, 3)

        piece_of = three.at[pl.ds(pl.multiple_of(peer * each, 16), each)]
        if o:
            copy = pltpu.make_async_remote_copy(
                src_ref=piece_of, dst_ref=slices_ref.at[band],
                send_sem=send_sem.at[base + o - 1], recv_sem=recv_sem.at[base + o - 1],
                device_id=band_device(o), device_id_type=MESH,
            )
            copy.start()
            swaps.append(copy)
        else:
            slices_ref[band] = piece_of[...]
    for copy in swaps:
        copy.wait()

    for i in range(count):
        row, col = place(i, 0, count)
        width = (i + 1) * BLK
        joined = jnp.concatenate([slices_ref[j] for j in range(i + 1)], 1)
        mine[row : row + BLK, col : col + width] = jnp.dot(
            slices_ref[i].T, joined, preferred_element_type=jnp.float32
        )

    copy = send(mine.at[rows_at((1 - core) * rows_half, rows_half)], from_core, other_core)
    copy.wait()
    half[...] = mine[rows_at(core * rows_half, rows_half), :] + from_core[...]

    copies = [
        send(half.at[rows_at(band_peer(o) * rows_band, rows_band)], from_band.at[o - 1], band_device(o))
        for o in range(1, bands)
    ]
    for copy in copies:
        copy.wait()
    summed = half[rows_at(band * rows_band, rows_band), :]
    for o in range(1, bands):
        summed = summed + from_band[o - 1]
    quarter[...] = summed

    copies = [
        send(quarter.at[rows_at(z_peer(o) * rows_z, rows_z)], from_z.at[o - 1], z_device(o))
        for o in range(1, levels)
    ]
    finish_ahead = send_ahead(
        range(0, 1), bands, band, cell, three, ahead_ref, send_sem, recv_sem, send_sem.shape[0] - bands + 1
    )
    for copy in copies:
        copy.wait()
    summed = quarter[rows_at(level * rows_z, rows_z), :]
    for o in range(1, levels):
        summed = summed + from_z[o - 1]
    summed = summed / total
    piece[...] = summed

    start_half = core * rows_half
    start_band = start_half + band * rows_band
    start_z = start_band + level * rows_z
    here = rows_at(start_z, rows_z)
    out_ref[here, :] = summed
    copies = [send(piece, out_ref.at[here], z_device(o)) for o in range(1, levels)]
    for copy in copies:
        copy.wait()
    here = out_ref.at[rows_at(start_band, rows_band)]
    copies = [send(here, here, band_device(o)) for o in range(1, bands)]
    for copy in copies:
        copy.wait()
    here = out_ref.at[rows_at(start_half, rows_half)]
    send(here, here, other_core).wait()
    finish_ahead()


def filtered(wavefunctions, stiffness, cell_scale, potential):
    bands, cells = lax.axis_size("band"), lax.axis_size("cell")
    band_rows, owned = wavefunctions.shape
    held = owned // OWN
    nodes = OWN + PLANE
    count = band_rows * bands // BLK
    each = owned // bands
    total = float(owned * cells)
    height, width = count * BLK // 2, (count + 1) * BLK
    levels = cells // 2
    rows_half = height // 2
    rows_band = rows_half // bands
    rows_z = rows_band // levels
    sends = 4 + 2 * (bands - 1) + 2 * (1 + (bands - 1) + (levels - 1))
    spans = owned + 5 * OWN + PLANE
    vmem = pl.BlockSpec(memory_space=pltpu.VMEM)
    f32, bf16 = jnp.float32, jnp.bfloat16
    return pl.pallas_call(
        functools.partial(filter_kernel, count, bands, cells, held, total),
        out_shape=(
            jax.ShapeDtypeStruct((bands, each, BLK), bf16),
            jax.ShapeDtypeStruct((owned, BLK), bf16),
            jax.ShapeDtypeStruct((bands - 1, 1, each, BLK), bf16),
            jax.ShapeDtypeStruct((height, width), f32),
        ),
        in_specs=[vmem] * 4,
        out_specs=(vmem,) * 4,
        scratch_shapes=[
            pltpu.VMEM((held, 1, nodes + BLK), f32),
            pltpu.VMEM((owned, BLK), bf16),
            pltpu.VMEM((spans, BLK), bf16),
            pltpu.VMEM((spans, BLK), bf16),
            pltpu.VMEM((spans, BLK), bf16),
            pltpu.VMEM((nodes, nodes), bf16),
            pltpu.VMEM((held + 5, 1, nodes + BLK), f32),
            pltpu.VMEM((held + 5, nodes, BLK), f32),
            pltpu.VMEM((height, width), f32),
            pltpu.VMEM((rows_half, width), f32),
            pltpu.VMEM((rows_half, width), f32),
            pltpu.VMEM((bands - 1, rows_band, width), f32),
            pltpu.VMEM((rows_band, width), f32),
            pltpu.VMEM((levels - 1, rows_z, width), f32),
            pltpu.VMEM((rows_z, width), f32),
            pltpu.SemaphoreType.DMA((sends,)),
            pltpu.SemaphoreType.DMA((sends,)),
        ],
        compiler_params=pltpu.CompilerParams(collective_id=0, has_side_effects=True),
    )(wavefunctions, stiffness, cell_scale[None, :], potential)


def rotate_kernel(bands, inverse_ref, slices_ref, own_ref, first_ref, rest_ref, out_ref):
    band = lax.axis_index("band")
    each = slices_ref.shape[1]
    for g in range(bands):

        @pl.when(band == g)
        def _():
            some = inverse_ref[g * BLK : (g + 1) * BLK, : (g + 1) * BLK]
            for r in range(bands):
                part = (g + r) % bands
                here = slice(part * each, (part + 1) * each)
                lower = lambda h: (
                    slices_ref[h] if r == 0 else first_ref[h, 0] if r == 1 else rest_ref[h, r - 2]
                )
                joined = jnp.concatenate([lower(h) for h in range(g)] + [own_ref[here, :]], 1)
                out_ref[:, here] = lax.dot_general(
                    some, joined, (((1,), (1,)), ((), ())), preferred_element_type=jnp.float32
                ).astype(out_ref.dtype)


def rotated_here(inverse, slices, own, first, rest):
    bands = slices.shape[0]
    vmem = pl.BlockSpec(memory_space=pltpu.VMEM)
    return pl.pallas_call(
        functools.partial(rotate_kernel, bands),
        out_shape=jax.ShapeDtypeStruct(own.shape[::-1], own.dtype),
        in_specs=[vmem] * 5,
        out_specs=vmem,
    )(inverse, slices, own, first, rest)


def fits(band_rows, owned, bands, cells):
    height = band_rows * bands // 2
    return (
        band_rows == BLK
        and owned % OWN == 0
        and bands >= 3
        and cells % 2 == 0
        and cells >= 4
        and owned // OWN >= 4
        and owned // OWN % (2 * bands) == 0
        and height % (16 * bands * (cells // 2)) == 0
    )


def margin_packed(slices):
    bands, cells = lax.axis_size("band"), lax.axis_size("cell")
    band_total, nodes = slices.shape
    count = band_total // BLK
    shape = jax.ShapeDtypeStruct((band_total // 2, (count + 1) * BLK), jnp.float32)
    vmem = pl.BlockSpec(memory_space=pltpu.VMEM)
    partial = pl.pallas_call(
        functools.partial(gram_kernel, count), out_shape=shape, in_specs=[vmem], out_specs=vmem
    )(slices)
    return lax.psum(partial, ("band", "cell")) / float(nodes * bands * cells)


def invert_block(block_ref):
    tiles = BLK // PAN
    shape = (PAN, BLK)
    lane = lax.broadcasted_iota(jnp.int32, (tiles, *shape), 2)
    line = lax.broadcasted_iota(jnp.int32, (tiles, *shape), 1)
    tile = lax.broadcasted_iota(jnp.int32, (tiles, *shape), 0)
    row = lax.broadcasted_iota(jnp.int32, shape, 0)
    left = block_ref[...].reshape(tiles, *shape)
    right = jnp.where(lane == line + tile * PAN, 1.0, 0.0).astype(jnp.float32)

    def spread(value):
        return jnp.broadcast_to(value, (1, *shape))

    for m in range(tiles):
        k = m * PAN
        now_left, now_right = left[0], right[0]
        more = m + 1 < tiles
        grid = [
            jnp.concatenate(
                [spread(now_left[i : i + 1, k + j : k + j + 1][None]) for i in range(j, PAN)], 0
            )
            for j in range(PAN)
        ]
        rows_left = jnp.concatenate([spread(now_left[j : j + 1, :][None]) for j in range(PAN)], 0)
        rows_right = jnp.concatenate([spread(now_right[j : j + 1, :][None]) for j in range(PAN)], 0)
        if more:
            left, right = left[1:], right[1:]
            cols = jnp.concatenate(
                [
                    jnp.broadcast_to(left[:, :, k + j : k + j + 1], left.shape)[None]
                    for j in range(PAN)
                ],
                0,
            )
        done = None
        for j in range(PAN):
            scale = lax.rsqrt(grid[j][0])
            head_left, head_right = rows_left[0] * scale, rows_right[0] * scale
            done = head_right if j == 0 else jnp.where(row == j, head_right, done)
            if j + 1 < PAN:
                factor = grid[j][1:] * scale
                for q in range(j + 1, PAN):
                    grid[q] = grid[q] - factor[q - j - 1 :] * factor[q - j - 1]
                rows_left = rows_left[1:] - factor * head_left
                rows_right = rows_right[1:] - factor * head_right
            if more:
                head = cols[0] * scale
                left = left - head * head_left
                right = right - head * head_right
                if j + 1 < PAN:
                    cols = cols[1:] - factor[:, None] * head[None]
        block_ref[k : k + PAN, :] = done


def exact(a, b, dims):
    return lax.dot_general(
        a, b, (dims, ((), ())), precision=lax.Precision.HIGHEST, preferred_element_type=jnp.float32
    )


NN = ((1,), (0,))
NT = ((1,), (1,))


def factor_kernel(
    count, bands, packed_ref, own_ref, out_ref, rest_ref, work, lower, inv, diag, send_sem, recv_sem
):
    band = lax.axis_index("band")
    cell = lax.axis_index("cell")
    barrier = pltpu.get_barrier_semaphore()
    for o in range(1, bands):
        device = {"band": lax.rem(band + o, bands), "cell": cell}
        pl.semaphore_signal(barrier, inc=1, device_id=device, device_id_type=MESH)
    pl.semaphore_wait(barrier, bands - 1)
    finish = send_ahead(
        range(1, bands - 1), bands, band, cell, own_ref, rest_ref, send_sem, recv_sem, 0
    )
    factor_steps(count, packed_ref, out_ref, work, lower, inv, diag)
    finish()


def factor_steps(count, packed_ref, out_ref, work, lower, inv, diag):
    size = count * BLK
    for i in range(count):
        row, col = place(i, 0, count)
        width = (i + 1) * BLK
        work[i * BLK : (i + 1) * BLK, :width] = packed_ref[row : row + BLK, col : col + width]
    inv[...] = jnp.zeros_like(inv)
    diag[...] = work[:BLK, :BLK]

    @pl.loop(0, count)
    def _(step):
        invert_block(diag)
        for j in range(count):

            @pl.when(step == j)
            def _():
                here = slice(j * BLK, (j + 1) * BLK)
                top = diag[...]
                if j:
                    partial = exact(lower[here, : j * BLK], inv[: j * BLK, : j * BLK], NN)
                    inv[here, : j * BLK] = -exact(top, partial, NN)
                inv[here, here] = top
                if j + 1 < count:
                    below = slice((j + 1) * BLK, size)
                    panel = exact(work[below, here], top, NT)
                    lower[below, here] = panel
                    work[below, below] = work[below, below] - exact(panel, panel, NT)
                    diag[...] = work[(j + 1) * BLK : (j + 2) * BLK, (j + 1) * BLK : (j + 2) * BLK]

    out_ref[...] = inv[...].astype(out_ref.dtype)


def inverse_factor(packed):
    size = packed.shape[0] * 2
    count = size // BLK
    vmem = pl.BlockSpec(memory_space=pltpu.VMEM)
    return pl.pallas_call(
        functools.partial(factor_steps, count),
        out_shape=jax.ShapeDtypeStruct((size, size), jnp.bfloat16),
        in_specs=[vmem],
        out_specs=vmem,
        scratch_shapes=[
            pltpu.VMEM((size, size), jnp.float32),
            pltpu.VMEM((size, size), jnp.float32),
            pltpu.VMEM((size, size), jnp.float32),
            pltpu.VMEM((BLK, BLK), jnp.float32),
        ],
    )(packed)


def inverse_and_rest(packed, own):
    bands = lax.axis_size("band")
    size = packed.shape[0] * 2
    count = size // BLK
    each = own.shape[0] // bands
    copies = (bands - 1) * (bands - 2)
    vmem = pl.BlockSpec(memory_space=pltpu.VMEM)
    return pl.pallas_call(
        functools.partial(factor_kernel, count, bands),
        out_shape=(
            jax.ShapeDtypeStruct((size, size), jnp.bfloat16),
            jax.ShapeDtypeStruct((bands - 1, bands - 2, each, BLK), own.dtype),
        ),
        in_specs=[vmem, vmem],
        out_specs=(vmem, vmem),
        scratch_shapes=[
            pltpu.VMEM((size, size), jnp.float32),
            pltpu.VMEM((size, size), jnp.float32),
            pltpu.VMEM((size, size), jnp.float32),
            pltpu.VMEM((BLK, BLK), jnp.float32),
            pltpu.SemaphoreType.DMA((copies,)),
            pltpu.SemaphoreType.DMA((copies,)),
        ],
        compiler_params=pltpu.CompilerParams(collective_id=1, has_side_effects=True),
    )(packed, own)


def shards(wavefunctions, stiffness, cell_scale, potential):
    if fits(*wavefunctions.shape, lax.axis_size("band"), lax.axis_size("cell")):
        slices, own, first, packed = filtered(wavefunctions, stiffness, cell_scale, potential)
        inverse, rest = inverse_and_rest(packed, own)
        return rotated_here(inverse, slices, own, first, rest)
    anchor = wavefunctions.astype(jnp.float32)
    degree_one = (
        (apply_h(wavefunctions, stiffness, cell_scale, potential) - centre * anchor) / half_width
    ).astype(jnp.bfloat16)
    one_wide = degree_one.astype(jnp.float32)
    degree_two = (
        2.0
        * (apply_h(degree_one, stiffness, cell_scale, potential) - centre * one_wide)
        / half_width
        - anchor
    ).astype(jnp.bfloat16)
    two_wide = degree_two.astype(jnp.float32)
    degree_three = (
        2.0
        * (apply_h(degree_two, stiffness, cell_scale, potential) - centre * two_wide)
        / half_width
        - one_wide
    ).astype(jnp.bfloat16)
    slices = lax.all_to_all(degree_three, "band", split_axis=1, concat_axis=0, tiled=True)
    inverse = inverse_factor(margin_packed(slices))
    rotated = jnp.dot(inverse, slices, preferred_element_type=jnp.float32).astype(jnp.bfloat16)
    return lax.all_to_all(rotated, "band", split_axis=0, concat_axis=1, tiled=True)


def solution(mesh):
    in_specs = (P("band", "cell"), P(), P("cell"), P("cell", None))
    out_specs = P("band", "cell")
    return jax.shard_map(shards, mesh=mesh, in_specs=in_specs, out_specs=out_specs, check_vma=False)
```

```python
import functools
import jax
import jax.numpy as jnp
from jax import lax
from jax.experimental import pallas as pl
from jax.experimental.pallas import tpu as pltpu
from jax.sharding import PartitionSpec as P

PLANE = 64
OWN = 448
BLK = 128
PAN = 8
MESH = pl.DeviceIdType.MESH

centre = 4.0
half_width = 3.0


def shifted(block, axis, distance):
    devices = range(lax.axis_size(axis))
    route = [((i - distance) % len(devices), i) for i in devices]
    return lax.ppermute(block, axis, route)


def apply_h(field, stiffness, cell_scale, potential):
    band_rows = field.shape[0]
    cell_count = field.shape[1] // OWN
    following = shifted(field[:, :PLANE], "cell", -1)
    owned_part = field.reshape(band_rows, cell_count, OWN)
    top_plane = jnp.concatenate([owned_part[:, 1:, :PLANE], following[:, None, :]], 1)
    cell_nodes = jnp.concatenate([owned_part, top_plane], 2)
    stiff_part = jnp.einsum(
        "bcn,nm->bcm", cell_nodes, stiffness, preferred_element_type=jnp.float32
    )
    cell_result = cell_scale[None, :, None] * stiff_part + potential[None] * cell_nodes.astype(
        jnp.float32
    )
    spill = cell_result[:, :, OWN:]
    incoming = shifted(spill[:, -1], "cell", 1)
    spill = jnp.concatenate([incoming[:, None, :], spill[:, :-1]], 1)
    kept = cell_result[:, :, :OWN]
    kept = jnp.concatenate([kept[:, :, :PLANE] + spill, kept[:, :, PLANE:]], 2)
    return kept.reshape(band_rows, cell_count * OWN)


def place(i, j, count):
    if i >= count // 2:
        return (count - 1 - i) * BLK, j * BLK
    return i * BLK, (count - i + j) * BLK


def packed_gram(slices_ref, packed_ref, count):
    for i in range(count):
        row, col = place(i, 0, count)
        width = (i + 1) * BLK
        packed_ref[row : row + BLK, col : col + width] = lax.dot_general(
            slices_ref[i * BLK : (i + 1) * BLK, :],
            slices_ref[:width, :],
            (((1,), (1,)), ((), ())),
            preferred_element_type=jnp.float32,
        )


def gram_kernel(count, slices_ref, packed_ref):
    packed_gram(slices_ref, packed_ref, count)


def rows_at(start, size):
    return pl.ds(pl.multiple_of(start, 8), size)


def pair_step(e, degree, source, older, target, st, potb, potx, shift=0):
    at = lambda c, skip, size: pl.ds(pl.multiple_of(c * OWN + skip, 16), size)
    nodes = OWN + PLANE
    va, vb = source[at(e, 0, nodes), :], source[at(e + 1, 0, nodes), :]
    vp = source[at(e - 1, 0, nodes), :]
    both = jnp.dot(st[...], jnp.concatenate([va, vb], 1), preferred_element_type=jnp.float32)
    before = jnp.dot(st[OWN:nodes, :], vp, preferred_element_type=jnp.float32)
    scale = lambda c: potx[c][:, nodes:]
    wa, wb = va.astype(jnp.float32), vb.astype(jnp.float32)
    ya = scale(e) * both[:, :BLK] + potb[e] * wa
    yb = scale(e + 1) * both[:, BLK:] + potb[e + 1] * wb
    yp = scale(e - 1) * before + potb[e - 1, OWN:, :] * vp[OWN:].astype(jnp.float32)

    def finish(c, h, w, skip):
        size = h.shape[0]
        value = h - centre * w
        if degree == 1:
            value = value * (1.0 / half_width)
        else:
            value = value * (2.0 / half_width) - older[at(c, skip, size), :].astype(jnp.float32)
        target[at(c - shift, skip, size), :] = value.astype(target.dtype)

    finish(e, ya[:PLANE] + yp, wa[:PLANE], 0)
    finish(e, ya[PLANE:OWN], wa[PLANE:OWN], PLANE)
    finish(e + 1, yb[:PLANE] + ya[OWN:], wb[:PLANE], 0)
    finish(e + 1, yb[PLANE:OWN], wb[PLANE:OWN], PLANE)


def send_ahead(turns, bands, band, cell, own_ref, ahead_ref, send_sem, recv_sem, base):
    each = ahead_ref.shape[2]
    wide = len(turns)
    device = lambda b: {"band": b, "cell": cell}

    def copy_to(b, n):
        part = (b + 1 + turns[n]) % bands
        return pltpu.make_async_remote_copy(
            src_ref=own_ref.at[part * each : (part + 1) * each], dst_ref=ahead_ref.at[band, n],
            send_sem=send_sem.at[base + (b - 1) * wide + n], recv_sem=recv_sem.at[base + band * wide + n],
            device_id=device(b), device_id_type=MESH,
        )

    def copy_from(h, n):
        return pltpu.make_async_remote_copy(
            src_ref=own_ref.at[0:each], dst_ref=ahead_ref.at[h, n],
            send_sem=send_sem.at[base + n], recv_sem=recv_sem.at[base + h * wide + n],
            device_id=device(h), device_id_type=MESH,
        )

    for n in range(wide):
        for b in range(1, bands):

            @pl.when(band < b)
            def _():
                copy_to(b, n).start()

    def finish():
        for n in range(wide):
            for b in range(1, bands):

                @pl.when(band < b)
                def _():
                    copy_to(b, n).wait_send()

                @pl.when(b - 1 < band)
                def _():
                    copy_from(b - 1, n).wait_recv()

    return finish


def filter_kernel(
    count, bands, cells, held, total,
    wave_ref, stiff_ref, scale_ref, potential_ref, slices_ref, three, ahead_ref, out_ref,
    pots, turned, ext, one, two, st, potx, potb,
    mine, from_core, half, from_band, quarter, from_z, piece,
    send_sem, recv_sem,
):
    band = lax.axis_index("band")
    cell = lax.axis_index("cell")
    core = lax.rem(cell, 2)
    level = lax.div(cell, 2)
    levels = cells // 2
    rows_half = mine.shape[0] // 2
    rows_band = rows_half // bands
    rows_z = rows_band // levels
    nodes = OWN + PLANE
    owned = held * OWN

    other_core = {"band": band, "cell": cell + 1 - 2 * core}
    band_peer = lambda o: lax.rem(band + o, bands)
    z_peer = lambda o: lax.rem(level + o, levels)
    band_device = lambda o: {"band": band_peer(o), "cell": cell}
    z_device = lambda o: {"band": band, "cell": z_peer(o) * 2 + core}
    cell_device = lambda o: {"band": band, "cell": lax.rem(cell + o, cells)}

    barrier = pltpu.get_barrier_semaphore()
    for o in range(1, bands):
        pl.semaphore_signal(barrier, inc=1, device_id=band_device(o), device_id_type=MESH)
    for o in range(1, cells):
        pl.semaphore_signal(barrier, inc=1, device_id=cell_device(o), device_id_type=MESH)
    used = [0]

    def send(src, dst, device):
        slot = used[0]
        used[0] += 1
        copy = pltpu.make_async_remote_copy(
            src_ref=src, dst_ref=dst, send_sem=send_sem.at[slot], recv_sem=recv_sem.at[slot],
            device_id=device, device_id_type=MESH,
        )
        copy.start()
        return copy

    low, high = 3 * OWN, 2 * OWN + PLANE
    right, left = cell_device(1), cell_device(cells - 1)

    def turn(q):
        span = slice(q * BLK, (q + 1) * BLK)
        turned[span, :] = wave_ref[:, span].T

    strips = owned // BLK
    first, last = -(-high // BLK), (owned - low) // BLK
    for c in range(held):
        pots[c, :, :nodes] = potential_ref[c : c + 1, :]
        pots[c, :, nodes:] = jnp.broadcast_to(scale_ref[:, c : c + 1], (1, BLK))
    for q in range(last, strips):
        turn(q)
    pl.semaphore_wait(barrier, bands - 1 + cells - 1)
    halo = [
        send(pots.at[held - 3 : held], potx.at[0:3], right),
        send(pots.at[0:2], potx.at[held + 3 : held + 5], left),
        send(turned.at[owned - low : owned], ext.at[0:low], right),
    ]
    for q in range(first):
        turn(q)
    halo.append(send(turned.at[0:high], ext.at[low + owned : low + owned + high], left))
    for q in range(first, last):
        turn(q)
    potx[3 : held + 3] = pots[...]
    ext[low : low + owned, :] = turned[...]
    st[...] = stiff_ref[...].T

    def columns(c):
        line = potx[c]
        for q in range(nodes // BLK):
            part = jnp.broadcast_to(line[:, q * BLK : (q + 1) * BLK], (BLK, BLK))
            potb[c, q * BLK : (q + 1) * BLK, :] = part.T

    @pl.loop(3, held + 3)
    def _(c):
        columns(c)

    @pl.loop(0, (held - 4) // 2)
    def _(p):
        pair_step(5 + 2 * p, 1, ext, None, one, st, potb, potx)

    for copy in halo:
        copy.wait()
    for c in (0, 1, 2, held + 3, held + 4):
        columns(c)

    @pl.loop(0, 4)
    def _(p):
        e = jnp.where(p < 2, 1 + 2 * p, held - 3 + 2 * p)
        pair_step(e, 1, ext, None, one, st, potb, potx)

    @pl.loop(0, held // 2 + 1)
    def _(p):
        pair_step(2 + 2 * p, 2, one, ext, two, st, potb, potx)

    each = owned // bands
    pairs = held // 2 // bands
    base = used[0]
    used[0] += bands - 1
    swaps = []
    for o in [*range(1, bands), 0]:
        peer = band_peer(o)

        @pl.loop(0, pairs)
        def _(p):
            pair_step(3 + 2 * (peer * pairs + p), 3, two, one, three, st, potb, potx, 3)

        piece_of = three.at[pl.ds(pl.multiple_of(peer * each, 16), each)]
        if o:
            copy = pltpu.make_async_remote_copy(
                src_ref=piece_of, dst_ref=slices_ref.at[band],
                send_sem=send_sem.at[base + o - 1], recv_sem=recv_sem.at[base + o - 1],
                device_id=band_device(o), device_id_type=MESH,
            )
            copy.start()
            swaps.append(copy)
        else:
            slices_ref[band] = piece_of[...]
    for copy in swaps:
        copy.wait()

    for i in range(count):
        row, col = place(i, 0, count)
        width = (i + 1) * BLK
        joined = jnp.concatenate([slices_ref[j] for j in range(i + 1)], 1)
        mine[row : row + BLK, col : col + width] = jnp.dot(
            slices_ref[i].T, joined, preferred_element_type=jnp.float32
        )

    cuts = [0, (count + 2) // 2 * BLK, (count + 1) * BLK]
    spans = [slice(cuts[n], cuts[n + 1]) for n in range(2)]
    start_half = core * rows_half
    start_band = start_half + band * rows_band
    start_z = start_band + level * rows_z

    def each_span(stage):
        return [stage(span) for span in spans]

    def wait_all(copies):
        for copy in copies:
            copy.wait()

    over_core = each_span(
        lambda span: [
            send(
                mine.at[rows_at((1 - core) * rows_half, rows_half), span],
                from_core.at[:, span],
                other_core,
            )
        ]
    )
    over_band = []
    for span, copies in zip(spans, over_core):
        wait_all(copies)
        half[:, span] = mine[rows_at(start_half, rows_half), span] + from_core[:, span]
        over_band.append([
            send(
                half.at[rows_at(band_peer(o) * rows_band, rows_band), span],
                from_band.at[o - 1, :, span],
                band_device(o),
            )
            for o in range(1, bands)
        ])
    over_z = []
    for span, copies in zip(spans, over_band):
        wait_all(copies)
        summed = half[rows_at(band * rows_band, rows_band), span]
        for o in range(1, bands):
            summed = summed + from_band[o - 1, :, span]
        quarter[:, span] = summed
        over_z.append([
            send(
                quarter.at[rows_at(z_peer(o) * rows_z, rows_z), span],
                from_z.at[o - 1, :, span],
                z_device(o),
            )
            for o in range(1, levels)
        ])
    finish_ahead = send_ahead(
        range(0, 1), bands, band, cell, three, ahead_ref, send_sem, recv_sem, send_sem.shape[0] - bands + 1
    )
    back_z = []
    for span, copies in zip(spans, over_z):
        wait_all(copies)
        summed = quarter[rows_at(level * rows_z, rows_z), span]
        for o in range(1, levels):
            summed = summed + from_z[o - 1, :, span]
        summed = summed / total
        piece[:, span] = summed
        here = rows_at(start_z, rows_z)
        out_ref[here, span] = summed
        back_z.append([
            send(piece.at[:, span], out_ref.at[here, span], z_device(o)) for o in range(1, levels)
        ])
    back_band = []
    for span, copies in zip(spans, back_z):
        wait_all(copies)
        here = out_ref.at[rows_at(start_band, rows_band), span]
        back_band.append([send(here, here, band_device(o)) for o in range(1, bands)])
    back_core = []
    for span, copies in zip(spans, back_band):
        wait_all(copies)
        here = out_ref.at[rows_at(start_half, rows_half), span]
        back_core.append([send(here, here, other_core)])
    for copies in back_core:
        wait_all(copies)
    finish_ahead()


def filtered(wavefunctions, stiffness, cell_scale, potential):
    bands, cells = lax.axis_size("band"), lax.axis_size("cell")
    band_rows, owned = wavefunctions.shape
    held = owned // OWN
    nodes = OWN + PLANE
    count = band_rows * bands // BLK
    each = owned // bands
    total = float(owned * cells)
    height, width = count * BLK // 2, (count + 1) * BLK
    levels = cells // 2
    rows_half = height // 2
    rows_band = rows_half // bands
    rows_z = rows_band // levels
    sends = 4 + 2 * (bands - 1) + 4 * (1 + (bands - 1) + (levels - 1))
    spans = owned + 5 * OWN + PLANE
    vmem = pl.BlockSpec(memory_space=pltpu.VMEM)
    f32, bf16 = jnp.float32, jnp.bfloat16
    return pl.pallas_call(
        functools.partial(filter_kernel, count, bands, cells, held, total),
        out_shape=(
            jax.ShapeDtypeStruct((bands, each, BLK), bf16),
            jax.ShapeDtypeStruct((owned, BLK), bf16),
            jax.ShapeDtypeStruct((bands - 1, 1, each, BLK), bf16),
            jax.ShapeDtypeStruct((height, width), f32),
        ),
        in_specs=[vmem] * 4,
        out_specs=(vmem,) * 4,
        scratch_shapes=[
            pltpu.VMEM((held, 1, nodes + BLK), f32),
            pltpu.VMEM((owned, BLK), bf16),
            pltpu.VMEM((spans, BLK), bf16),
            pltpu.VMEM((spans, BLK), bf16),
            pltpu.VMEM((spans, BLK), bf16),
            pltpu.VMEM((nodes, nodes), bf16),
            pltpu.VMEM((held + 5, 1, nodes + BLK), f32),
            pltpu.VMEM((held + 5, nodes, BLK), f32),
            pltpu.VMEM((height, width), f32),
            pltpu.VMEM((rows_half, width), f32),
            pltpu.VMEM((rows_half, width), f32),
            pltpu.VMEM((bands - 1, rows_band, width), f32),
            pltpu.VMEM((rows_band, width), f32),
            pltpu.VMEM((levels - 1, rows_z, width), f32),
            pltpu.VMEM((rows_z, width), f32),
            pltpu.SemaphoreType.DMA((sends,)),
            pltpu.SemaphoreType.DMA((sends,)),
        ],
        compiler_params=pltpu.CompilerParams(collective_id=0, has_side_effects=True),
    )(wavefunctions, stiffness, cell_scale[None, :], potential)


def rotate_kernel(bands, inverse_ref, slices_ref, own_ref, first_ref, rest_ref, out_ref):
    band = lax.axis_index("band")
    each = slices_ref.shape[1]
    for g in range(bands):

        @pl.when(band == g)
        def _():
            some = inverse_ref[g * BLK : (g + 1) * BLK, : (g + 1) * BLK]
            for r in range(bands):
                part = (g + r) % bands
                here = slice(part * each, (part + 1) * each)
                lower = lambda h: (
                    slices_ref[h] if r == 0 else first_ref[h, 0] if r == 1 else rest_ref[h, r - 2]
                )
                joined = jnp.concatenate([lower(h) for h in range(g)] + [own_ref[here, :]], 1)
                out_ref[:, here] = lax.dot_general(
                    some, joined, (((1,), (1,)), ((), ())), preferred_element_type=jnp.float32
                ).astype(out_ref.dtype)


def rotated_here(inverse, slices, own, first, rest):
    bands = slices.shape[0]
    vmem = pl.BlockSpec(memory_space=pltpu.VMEM)
    return pl.pallas_call(
        functools.partial(rotate_kernel, bands),
        out_shape=jax.ShapeDtypeStruct(own.shape[::-1], own.dtype),
        in_specs=[vmem] * 5,
        out_specs=vmem,
    )(inverse, slices, own, first, rest)


def fits(band_rows, owned, bands, cells):
    height = band_rows * bands // 2
    return (
        band_rows == BLK
        and owned % OWN == 0
        and bands >= 3
        and cells % 2 == 0
        and cells >= 4
        and owned // OWN >= 4
        and owned // OWN % (2 * bands) == 0
        and height % (16 * bands * (cells // 2)) == 0
    )


def margin_packed(slices):
    bands, cells = lax.axis_size("band"), lax.axis_size("cell")
    band_total, nodes = slices.shape
    count = band_total // BLK
    shape = jax.ShapeDtypeStruct((band_total // 2, (count + 1) * BLK), jnp.float32)
    vmem = pl.BlockSpec(memory_space=pltpu.VMEM)
    partial = pl.pallas_call(
        functools.partial(gram_kernel, count), out_shape=shape, in_specs=[vmem], out_specs=vmem
    )(slices)
    return lax.psum(partial, ("band", "cell")) / float(nodes * bands * cells)


def invert_block(block_ref):
    tiles = BLK // PAN
    shape = (PAN, BLK)
    lane = lax.broadcasted_iota(jnp.int32, (tiles, *shape), 2)
    line = lax.broadcasted_iota(jnp.int32, (tiles, *shape), 1)
    tile = lax.broadcasted_iota(jnp.int32, (tiles, *shape), 0)
    row = lax.broadcasted_iota(jnp.int32, shape, 0)
    left = block_ref[...].reshape(tiles, *shape)
    right = jnp.where(lane == line + tile * PAN, 1.0, 0.0).astype(jnp.float32)

    def spread(value):
        return jnp.broadcast_to(value, (1, *shape))

    for m in range(tiles):
        k = m * PAN
        now_left, now_right = left[0], right[0]
        more = m + 1 < tiles
        grid = [
            jnp.concatenate(
                [spread(now_left[i : i + 1, k + j : k + j + 1][None]) for i in range(j, PAN)], 0
            )
            for j in range(PAN)
        ]
        rows_left = jnp.concatenate([spread(now_left[j : j + 1, :][None]) for j in range(PAN)], 0)
        rows_right = jnp.concatenate([spread(now_right[j : j + 1, :][None]) for j in range(PAN)], 0)
        if more:
            left, right = left[1:], right[1:]
            cols = jnp.concatenate(
                [
                    jnp.broadcast_to(left[:, :, k + j : k + j + 1], left.shape)[None]
                    for j in range(PAN)
                ],
                0,
            )
        done = None
        for j in range(PAN):
            scale = lax.rsqrt(grid[j][0])
            head_left, head_right = rows_left[0] * scale, rows_right[0] * scale
            done = head_right if j == 0 else jnp.where(row == j, head_right, done)
            if j + 1 < PAN:
                factor = grid[j][1:] * scale
                for q in range(j + 1, PAN):
                    grid[q] = grid[q] - factor[q - j - 1 :] * factor[q - j - 1]
                rows_left = rows_left[1:] - factor * head_left
                rows_right = rows_right[1:] - factor * head_right
            if more:
                head = cols[0] * scale
                left = left - head * head_left
                right = right - head * head_right
                if j + 1 < PAN:
                    cols = cols[1:] - factor[:, None] * head[None]
        block_ref[k : k + PAN, :] = done


def exact(a, b, dims):
    return lax.dot_general(
        a, b, (dims, ((), ())), precision=lax.Precision.HIGHEST, preferred_element_type=jnp.float32
    )


NN = ((1,), (0,))
NT = ((1,), (1,))


def factor_kernel(
    count, bands, packed_ref, own_ref, out_ref, rest_ref, work, lower, inv, diag, send_sem, recv_sem
):
    band = lax.axis_index("band")
    cell = lax.axis_index("cell")
    barrier = pltpu.get_barrier_semaphore()
    for o in range(1, bands):
        device = {"band": lax.rem(band + o, bands), "cell": cell}
        pl.semaphore_signal(barrier, inc=1, device_id=device, device_id_type=MESH)
    pl.semaphore_wait(barrier, bands - 1)
    finish = send_ahead(
        range(1, bands - 1), bands, band, cell, own_ref, rest_ref, send_sem, recv_sem, 0
    )
    factor_steps(count, packed_ref, out_ref, work, lower, inv, diag)
    finish()


def factor_steps(count, packed_ref, out_ref, work, lower, inv, diag):
    size = count * BLK
    for i in range(count):
        row, col = place(i, 0, count)
        width = (i + 1) * BLK
        work[i * BLK : (i + 1) * BLK, :width] = packed_ref[row : row + BLK, col : col + width]
    inv[...] = jnp.zeros_like(inv)
    block = lambda i: slice(i * BLK, (i + 1) * BLK)
    diag[0] = work[:BLK, :BLK]
    invert_block(diag.at[0])
    for j in range(count):
        here, top = block(j), diag[j]
        if j + 1 < count:
            ahead = block(j + 1)
            panel = exact(work[ahead, here], top, NT)
            lower[ahead, here] = panel
            diag[j + 1] = work[ahead, ahead] - exact(panel, panel, NT)
            invert_block(diag.at[j + 1])
            for i in range(j + 2, count):
                lower[block(i), here] = exact(work[block(i), here], top, NT)
                for q in range(j + 1, i + 1):
                    work[block(i), block(q)] = work[block(i), block(q)] - exact(
                        lower[block(i), here], lower[block(q), here], NT
                    )
        if j:
            partial = exact(lower[here, : j * BLK], inv[: j * BLK, : j * BLK], NN)
            inv[here, : j * BLK] = -exact(top, partial, NN)
        inv[here, here] = top

    out_ref[...] = inv[...].astype(out_ref.dtype)


def inverse_factor(packed):
    size = packed.shape[0] * 2
    count = size // BLK
    vmem = pl.BlockSpec(memory_space=pltpu.VMEM)
    return pl.pallas_call(
        functools.partial(factor_steps, count),
        out_shape=jax.ShapeDtypeStruct((size, size), jnp.bfloat16),
        in_specs=[vmem],
        out_specs=vmem,
        scratch_shapes=[
            pltpu.VMEM((size, size), jnp.float32),
            pltpu.VMEM((size, size), jnp.float32),
            pltpu.VMEM((size, size), jnp.float32),
            pltpu.VMEM((count, BLK, BLK), jnp.float32),
        ],
    )(packed)


def inverse_and_rest(packed, own):
    bands = lax.axis_size("band")
    size = packed.shape[0] * 2
    count = size // BLK
    each = own.shape[0] // bands
    copies = (bands - 1) * (bands - 2)
    vmem = pl.BlockSpec(memory_space=pltpu.VMEM)
    return pl.pallas_call(
        functools.partial(factor_kernel, count, bands),
        out_shape=(
            jax.ShapeDtypeStruct((size, size), jnp.bfloat16),
            jax.ShapeDtypeStruct((bands - 1, bands - 2, each, BLK), own.dtype),
        ),
        in_specs=[vmem, vmem],
        out_specs=(vmem, vmem),
        scratch_shapes=[
            pltpu.VMEM((size, size), jnp.float32),
            pltpu.VMEM((size, size), jnp.float32),
            pltpu.VMEM((size, size), jnp.float32),
            pltpu.VMEM((count, BLK, BLK), jnp.float32),
            pltpu.SemaphoreType.DMA((copies,)),
            pltpu.SemaphoreType.DMA((copies,)),
        ],
        compiler_params=pltpu.CompilerParams(collective_id=1, has_side_effects=True),
    )(packed, own)


def shards(wavefunctions, stiffness, cell_scale, potential):
    if fits(*wavefunctions.shape, lax.axis_size("band"), lax.axis_size("cell")):
        slices, own, first, packed = filtered(wavefunctions, stiffness, cell_scale, potential)
        inverse, rest = inverse_and_rest(packed, own)
        return rotated_here(inverse, slices, own, first, rest)
    anchor = wavefunctions.astype(jnp.float32)
    degree_one = (
        (apply_h(wavefunctions, stiffness, cell_scale, potential) - centre * anchor) / half_width
    ).astype(jnp.bfloat16)
    one_wide = degree_one.astype(jnp.float32)
    degree_two = (
        2.0
        * (apply_h(degree_one, stiffness, cell_scale, potential) - centre * one_wide)
        / half_width
        - anchor
    ).astype(jnp.bfloat16)
    two_wide = degree_two.astype(jnp.float32)
    degree_three = (
        2.0
        * (apply_h(degree_two, stiffness, cell_scale, potential) - centre * two_wide)
        / half_width
        - one_wide
    ).astype(jnp.bfloat16)
    slices = lax.all_to_all(degree_three, "band", split_axis=1, concat_axis=0, tiled=True)
    inverse = inverse_factor(margin_packed(slices))
    rotated = jnp.dot(inverse, slices, preferred_element_type=jnp.float32).astype(jnp.bfloat16)
    return lax.all_to_all(rotated, "band", split_axis=0, concat_axis=1, tiled=True)


def solution(mesh):
    in_specs = (P("band", "cell"), P(), P("cell"), P("cell", None))
    out_specs = P("band", "cell")
    return jax.shard_map(shards, mesh=mesh, in_specs=in_specs, out_specs=out_specs, check_vma=False)
```

```python
import functools
import jax
import jax.numpy as jnp
from jax import lax
from jax.experimental import pallas as pl
from jax.experimental.pallas import tpu as pltpu
from jax.sharding import PartitionSpec as P

PLANE = 64
OWN = 448
BLK = 128
PAN = 8
MESH = pl.DeviceIdType.MESH

centre = 4.0
half_width = 3.0


def shifted(block, axis, distance):
    devices = range(lax.axis_size(axis))
    route = [((i - distance) % len(devices), i) for i in devices]
    return lax.ppermute(block, axis, route)


def apply_h(field, stiffness, cell_scale, potential):
    band_rows = field.shape[0]
    cell_count = field.shape[1] // OWN
    following = shifted(field[:, :PLANE], "cell", -1)
    owned_part = field.reshape(band_rows, cell_count, OWN)
    top_plane = jnp.concatenate([owned_part[:, 1:, :PLANE], following[:, None, :]], 1)
    cell_nodes = jnp.concatenate([owned_part, top_plane], 2)
    stiff_part = jnp.einsum(
        "bcn,nm->bcm", cell_nodes, stiffness, preferred_element_type=jnp.float32
    )
    cell_result = cell_scale[None, :, None] * stiff_part + potential[None] * cell_nodes.astype(
        jnp.float32
    )
    spill = cell_result[:, :, OWN:]
    incoming = shifted(spill[:, -1], "cell", 1)
    spill = jnp.concatenate([incoming[:, None, :], spill[:, :-1]], 1)
    kept = cell_result[:, :, :OWN]
    kept = jnp.concatenate([kept[:, :, :PLANE] + spill, kept[:, :, PLANE:]], 2)
    return kept.reshape(band_rows, cell_count * OWN)


def place(i, j, count):
    if i >= count // 2:
        return (count - 1 - i) * BLK, j * BLK
    return i * BLK, (count - i + j) * BLK


def packed_gram(slices_ref, packed_ref, count):
    for i in range(count):
        row, col = place(i, 0, count)
        width = (i + 1) * BLK
        packed_ref[row : row + BLK, col : col + width] = lax.dot_general(
            slices_ref[i * BLK : (i + 1) * BLK, :],
            slices_ref[:width, :],
            (((1,), (1,)), ((), ())),
            preferred_element_type=jnp.float32,
        )


def gram_kernel(count, slices_ref, packed_ref):
    packed_gram(slices_ref, packed_ref, count)


def rows_at(start, size):
    return pl.ds(pl.multiple_of(start, 8), size)


def pair_step(e, degree, source, older, target, st, potb, potx, shift=0):
    at = lambda c, skip, size: pl.ds(pl.multiple_of(c * OWN + skip, 16), size)
    nodes = OWN + PLANE
    va, vb = source[at(e, 0, nodes), :], source[at(e + 1, 0, nodes), :]
    vp = source[at(e - 1, 0, nodes), :]
    both = jnp.dot(st[...], jnp.concatenate([va, vb], 1), preferred_element_type=jnp.float32)
    before = jnp.dot(st[OWN:nodes, :], vp, preferred_element_type=jnp.float32)
    scale = lambda c: potx[c][:, nodes:]
    wa, wb = va.astype(jnp.float32), vb.astype(jnp.float32)
    ya = scale(e) * both[:, :BLK] + potb[e] * wa
    yb = scale(e + 1) * both[:, BLK:] + potb[e + 1] * wb
    yp = scale(e - 1) * before + potb[e - 1, OWN:, :] * vp[OWN:].astype(jnp.float32)

    def finish(c, h, w, skip):
        size = h.shape[0]
        value = h - centre * w
        if degree == 1:
            value = value * (1.0 / half_width)
        else:
            value = value * (2.0 / half_width) - older[at(c, skip, size), :].astype(jnp.float32)
        target[at(c - shift, skip, size), :] = value.astype(target.dtype)

    finish(e, ya[:PLANE] + yp, wa[:PLANE], 0)
    finish(e, ya[PLANE:OWN], wa[PLANE:OWN], PLANE)
    finish(e + 1, yb[:PLANE] + ya[OWN:], wb[:PLANE], 0)
    finish(e + 1, yb[PLANE:OWN], wb[PLANE:OWN], PLANE)


def send_ahead(turns, bands, band, cell, own_ref, ahead_ref, send_sem, recv_sem, base):
    each = ahead_ref.shape[2]
    wide = len(turns)
    device = lambda b: {"band": b, "cell": cell}

    def copy_to(b, n):
        part = (b + 1 + turns[n]) % bands
        return pltpu.make_async_remote_copy(
            src_ref=own_ref.at[part * each : (part + 1) * each], dst_ref=ahead_ref.at[band, n],
            send_sem=send_sem.at[base + (b - 1) * wide + n], recv_sem=recv_sem.at[base + band * wide + n],
            device_id=device(b), device_id_type=MESH,
        )

    def copy_from(h, n):
        return pltpu.make_async_remote_copy(
            src_ref=own_ref.at[0:each], dst_ref=ahead_ref.at[h, n],
            send_sem=send_sem.at[base + n], recv_sem=recv_sem.at[base + h * wide + n],
            device_id=device(h), device_id_type=MESH,
        )

    for n in range(wide):
        for b in range(1, bands):

            @pl.when(band < b)
            def _():
                copy_to(b, n).start()

    def finish():
        for n in range(wide):
            for b in range(1, bands):

                @pl.when(band < b)
                def _():
                    copy_to(b, n).wait_send()

                @pl.when(b - 1 < band)
                def _():
                    copy_from(b - 1, n).wait_recv()

    return finish


def filter_kernel(
    count, bands, cells, held, total,
    wave_ref, stiff_ref, scale_ref, potential_ref, slices_ref, three, ahead_ref, out_ref,
    pots, turned, ext, one, two, st, potx, potb,
    mine, from_core, half, from_band, quarter, from_z, piece,
    send_sem, recv_sem,
):
    band = lax.axis_index("band")
    cell = lax.axis_index("cell")
    core = lax.rem(cell, 2)
    level = lax.div(cell, 2)
    levels = cells // 2
    rows_half = mine.shape[0] // 2
    rows_band = rows_half // bands
    rows_z = rows_band // levels
    nodes = OWN + PLANE
    owned = held * OWN

    other_core = {"band": band, "cell": cell + 1 - 2 * core}
    band_peer = lambda o: lax.rem(band + o, bands)
    z_peer = lambda o: lax.rem(level + o, levels)
    band_device = lambda o: {"band": band_peer(o), "cell": cell}
    z_device = lambda o: {"band": band, "cell": z_peer(o) * 2 + core}
    cell_device = lambda o: {"band": band, "cell": lax.rem(cell + o, cells)}

    barrier = pltpu.get_barrier_semaphore()
    for o in range(1, bands):
        pl.semaphore_signal(barrier, inc=1, device_id=band_device(o), device_id_type=MESH)
    for o in range(1, cells):
        pl.semaphore_signal(barrier, inc=1, device_id=cell_device(o), device_id_type=MESH)
    used = [0]

    def send(src, dst, device):
        slot = used[0]
        used[0] += 1
        copy = pltpu.make_async_remote_copy(
            src_ref=src, dst_ref=dst, send_sem=send_sem.at[slot], recv_sem=recv_sem.at[slot],
            device_id=device, device_id_type=MESH,
        )
        copy.start()
        return copy

    low, high = 3 * OWN, 2 * OWN + PLANE
    right, left = cell_device(1), cell_device(cells - 1)

    def turn(q):
        span = slice(q * BLK, (q + 1) * BLK)
        turned[span, :] = wave_ref[:, span].T

    strips = owned // BLK
    first, last = -(-high // BLK), (owned - low) // BLK
    for c in range(held):
        pots[c, :, :nodes] = potential_ref[c : c + 1, :]
        pots[c, :, nodes:] = jnp.broadcast_to(scale_ref[:, c : c + 1], (1, BLK))
    for q in range(last, strips):
        turn(q)
    pl.semaphore_wait(barrier, bands - 1 + cells - 1)
    halo = [
        send(pots.at[held - 3 : held], potx.at[0:3], right),
        send(pots.at[0:2], potx.at[held + 3 : held + 5], left),
        send(turned.at[owned - low : owned], ext.at[0:low], right),
    ]
    for q in range(first):
        turn(q)
    halo.append(send(turned.at[0:high], ext.at[low + owned : low + owned + high], left))
    for q in range(first, last):
        turn(q)
    potx[3 : held + 3] = pots[...]
    ext[low : low + owned, :] = turned[...]
    st[...] = stiff_ref[...].T

    def columns(c):
        line = potx[c]
        for q in range(nodes // BLK):
            part = jnp.broadcast_to(line[:, q * BLK : (q + 1) * BLK], (BLK, BLK))
            potb[c, q * BLK : (q + 1) * BLK, :] = part.T

    @pl.loop(3, held + 3)
    def _(c):
        columns(c)

    @pl.loop(0, (held - 4) // 2)
    def _(p):
        pair_step(5 + 2 * p, 1, ext, None, one, st, potb, potx)

    for copy in halo:
        copy.wait()
    for c in (0, 1, 2, held + 3, held + 4):
        columns(c)

    @pl.loop(0, 4)
    def _(p):
        e = jnp.where(p < 2, 1 + 2 * p, held - 3 + 2 * p)
        pair_step(e, 1, ext, None, one, st, potb, potx)

    @pl.loop(0, held // 2 + 1)
    def _(p):
        pair_step(2 + 2 * p, 2, one, ext, two, st, potb, potx)

    each = owned // bands
    pairs = held // 2 // bands
    base = used[0]
    used[0] += bands - 1
    swaps = []
    for o in [*range(1, bands), 0]:
        peer = band_peer(o)

        @pl.loop(0, pairs)
        def _(p):
            pair_step(3 + 2 * (peer * pairs + p), 3, two, one, three, st, potb, potx, 3)

        piece_of = three.at[pl.ds(pl.multiple_of(peer * each, 16), each)]
        if o:
            copy = pltpu.make_async_remote_copy(
                src_ref=piece_of, dst_ref=slices_ref.at[band],
                send_sem=send_sem.at[base + o - 1], recv_sem=recv_sem.at[base + o - 1],
                device_id=band_device(o), device_id_type=MESH,
            )
            copy.start()
            swaps.append(copy)
        else:
            slices_ref[band] = piece_of[...]
    for copy in swaps:
        copy.wait()
    finish_ahead = send_ahead(
        range(0, 1), bands, band, cell, three, ahead_ref, send_sem, recv_sem, send_sem.shape[0] - bands + 1
    )

    for i in range(count):
        row, col = place(i, 0, count)
        width = (i + 1) * BLK
        joined = jnp.concatenate([slices_ref[j] for j in range(i + 1)], 1)
        mine[row : row + BLK, col : col + width] = jnp.dot(
            slices_ref[i].T, joined, preferred_element_type=jnp.float32
        )

    cuts = [0, (count + 2) // 2 * BLK, (count + 1) * BLK]
    spans = [slice(cuts[n], cuts[n + 1]) for n in range(2)]
    start_half = core * rows_half
    start_band = start_half + band * rows_band
    start_z = start_band + level * rows_z

    def each_span(stage):
        return [stage(span) for span in spans]

    def wait_all(copies):
        for copy in copies:
            copy.wait()

    over_core = each_span(
        lambda span: [
            send(
                mine.at[rows_at((1 - core) * rows_half, rows_half), span],
                from_core.at[:, span],
                other_core,
            )
        ]
    )
    over_band = []
    for span, copies in zip(spans, over_core):
        wait_all(copies)
        half[:, span] = mine[rows_at(start_half, rows_half), span] + from_core[:, span]
        over_band.append([
            send(
                half.at[rows_at(band_peer(o) * rows_band, rows_band), span],
                from_band.at[o - 1, :, span],
                band_device(o),
            )
            for o in range(1, bands)
        ])
    over_z = []
    for span, copies in zip(spans, over_band):
        wait_all(copies)
        summed = half[rows_at(band * rows_band, rows_band), span]
        for o in range(1, bands):
            summed = summed + from_band[o - 1, :, span]
        quarter[:, span] = summed
        over_z.append([
            send(
                quarter.at[rows_at(z_peer(o) * rows_z, rows_z), span],
                from_z.at[o - 1, :, span],
                z_device(o),
            )
            for o in range(1, levels)
        ])
    back_z = []
    for span, copies in zip(spans, over_z):
        wait_all(copies)
        summed = quarter[rows_at(level * rows_z, rows_z), span]
        for o in range(1, levels):
            summed = summed + from_z[o - 1, :, span]
        summed = summed / total
        piece[:, span] = summed
        here = rows_at(start_z, rows_z)
        out_ref[here, span] = summed
        back_z.append([
            send(piece.at[:, span], out_ref.at[here, span], z_device(o)) for o in range(1, levels)
        ])
    back_band = []
    for span, copies in zip(spans, back_z):
        wait_all(copies)
        here = out_ref.at[rows_at(start_band, rows_band), span]
        back_band.append([send(here, here, band_device(o)) for o in range(1, bands)])
    back_core = []
    for span, copies in zip(spans, back_band):
        wait_all(copies)
        here = out_ref.at[rows_at(start_half, rows_half), span]
        back_core.append([send(here, here, other_core)])
    for copies in back_core:
        wait_all(copies)
    finish_ahead()


def filtered(wavefunctions, stiffness, cell_scale, potential):
    bands, cells = lax.axis_size("band"), lax.axis_size("cell")
    band_rows, owned = wavefunctions.shape
    held = owned // OWN
    nodes = OWN + PLANE
    count = band_rows * bands // BLK
    each = owned // bands
    total = float(owned * cells)
    height, width = count * BLK // 2, (count + 1) * BLK
    levels = cells // 2
    rows_half = height // 2
    rows_band = rows_half // bands
    rows_z = rows_band // levels
    sends = 4 + 2 * (bands - 1) + 4 * (1 + (bands - 1) + (levels - 1))
    spans = owned + 5 * OWN + PLANE
    vmem = pl.BlockSpec(memory_space=pltpu.VMEM)
    f32, bf16 = jnp.float32, jnp.bfloat16
    return pl.pallas_call(
        functools.partial(filter_kernel, count, bands, cells, held, total),
        out_shape=(
            jax.ShapeDtypeStruct((bands, each, BLK), bf16),
            jax.ShapeDtypeStruct((owned, BLK), bf16),
            jax.ShapeDtypeStruct((bands - 1, 1, each, BLK), bf16),
            jax.ShapeDtypeStruct((height, width), f32),
        ),
        in_specs=[vmem] * 4,
        out_specs=(vmem,) * 4,
        scratch_shapes=[
            pltpu.VMEM((held, 1, nodes + BLK), f32),
            pltpu.VMEM((owned, BLK), bf16),
            pltpu.VMEM((spans, BLK), bf16),
            pltpu.VMEM((spans, BLK), bf16),
            pltpu.VMEM((spans, BLK), bf16),
            pltpu.VMEM((nodes, nodes), bf16),
            pltpu.VMEM((held + 5, 1, nodes + BLK), f32),
            pltpu.VMEM((held + 5, nodes, BLK), f32),
            pltpu.VMEM((height, width), f32),
            pltpu.VMEM((rows_half, width), f32),
            pltpu.VMEM((rows_half, width), f32),
            pltpu.VMEM((bands - 1, rows_band, width), f32),
            pltpu.VMEM((rows_band, width), f32),
            pltpu.VMEM((levels - 1, rows_z, width), f32),
            pltpu.VMEM((rows_z, width), f32),
            pltpu.SemaphoreType.DMA((sends,)),
            pltpu.SemaphoreType.DMA((sends,)),
        ],
        compiler_params=pltpu.CompilerParams(collective_id=0, has_side_effects=True),
    )(wavefunctions, stiffness, cell_scale[None, :], potential)


def rotate_kernel(bands, inverse_ref, slices_ref, own_ref, first_ref, rest_ref, out_ref):
    band = lax.axis_index("band")
    each = slices_ref.shape[1]
    for g in range(bands):

        @pl.when(band == g)
        def _():
            some = inverse_ref[g * BLK : (g + 1) * BLK, : (g + 1) * BLK]
            for r in range(bands):
                part = (g + r) % bands
                here = slice(part * each, (part + 1) * each)
                lower = lambda h: (
                    slices_ref[h] if r == 0 else first_ref[h, 0] if r == 1 else rest_ref[h, r - 2]
                )
                joined = jnp.concatenate([lower(h) for h in range(g)] + [own_ref[here, :]], 1)
                out_ref[:, here] = lax.dot_general(
                    some, joined, (((1,), (1,)), ((), ())), preferred_element_type=jnp.float32
                ).astype(out_ref.dtype)


def rotated_here(inverse, slices, own, first, rest):
    bands = slices.shape[0]
    vmem = pl.BlockSpec(memory_space=pltpu.VMEM)
    return pl.pallas_call(
        functools.partial(rotate_kernel, bands),
        out_shape=jax.ShapeDtypeStruct(own.shape[::-1], own.dtype),
        in_specs=[vmem] * 5,
        out_specs=vmem,
    )(inverse, slices, own, first, rest)


def fits(band_rows, owned, bands, cells):
    height = band_rows * bands // 2
    return (
        band_rows == BLK
        and owned % OWN == 0
        and bands >= 3
        and cells % 2 == 0
        and cells >= 4
        and owned // OWN >= 4
        and owned // OWN % (2 * bands) == 0
        and height % (16 * bands * (cells // 2)) == 0
    )


def margin_packed(slices):
    bands, cells = lax.axis_size("band"), lax.axis_size("cell")
    band_total, nodes = slices.shape
    count = band_total // BLK
    shape = jax.ShapeDtypeStruct((band_total // 2, (count + 1) * BLK), jnp.float32)
    vmem = pl.BlockSpec(memory_space=pltpu.VMEM)
    partial = pl.pallas_call(
        functools.partial(gram_kernel, count), out_shape=shape, in_specs=[vmem], out_specs=vmem
    )(slices)
    return lax.psum(partial, ("band", "cell")) / float(nodes * bands * cells)


def invert_block(block_ref):
    tiles = BLK // PAN
    shape = (PAN, BLK)
    lane = lax.broadcasted_iota(jnp.int32, (tiles, *shape), 2)
    line = lax.broadcasted_iota(jnp.int32, (tiles, *shape), 1)
    tile = lax.broadcasted_iota(jnp.int32, (tiles, *shape), 0)
    row = lax.broadcasted_iota(jnp.int32, shape, 0)
    left = block_ref[...].reshape(tiles, *shape)
    right = jnp.where(lane == line + tile * PAN, 1.0, 0.0).astype(jnp.float32)

    def spread(value):
        return jnp.broadcast_to(value, (1, *shape))

    for m in range(tiles):
        k = m * PAN
        now_left, now_right = left[0], right[0]
        more = m + 1 < tiles
        grid = [
            jnp.concatenate(
                [spread(now_left[i : i + 1, k + j : k + j + 1][None]) for i in range(j, PAN)], 0
            )
            for j in range(PAN)
        ]
        rows_left = jnp.concatenate([spread(now_left[j : j + 1, :][None]) for j in range(PAN)], 0)
        rows_right = jnp.concatenate([spread(now_right[j : j + 1, :][None]) for j in range(PAN)], 0)
        if more:
            left, right = left[1:], right[1:]
            cols = jnp.concatenate(
                [
                    jnp.broadcast_to(left[:, :, k + j : k + j + 1], left.shape)[None]
                    for j in range(PAN)
                ],
                0,
            )
        done = None
        for j in range(PAN):
            scale = lax.rsqrt(grid[j][0])
            head_left, head_right = rows_left[0] * scale, rows_right[0] * scale
            done = head_right if j == 0 else jnp.where(row == j, head_right, done)
            if j + 1 < PAN:
                factor = grid[j][1:] * scale
                for q in range(j + 1, PAN):
                    grid[q] = grid[q] - factor[q - j - 1 :] * factor[q - j - 1]
                rows_left = rows_left[1:] - factor * head_left
                rows_right = rows_right[1:] - factor * head_right
            if more:
                head = cols[0] * scale
                left = left - head * head_left
                right = right - head * head_right
                if j + 1 < PAN:
                    cols = cols[1:] - factor[:, None] * head[None]
        block_ref[k : k + PAN, :] = done


def exact(a, b, dims):
    return lax.dot_general(
        a, b, (dims, ((), ())), precision=lax.Precision.HIGHEST, preferred_element_type=jnp.float32
    )


NN = ((1,), (0,))
NT = ((1,), (1,))


def factor_kernel(
    count, bands, packed_ref, own_ref, out_ref, rest_ref, work, lower, inv, diag, send_sem, recv_sem
):
    band = lax.axis_index("band")
    cell = lax.axis_index("cell")
    barrier = pltpu.get_barrier_semaphore()
    for o in range(1, bands):
        device = {"band": lax.rem(band + o, bands), "cell": cell}
        pl.semaphore_signal(barrier, inc=1, device_id=device, device_id_type=MESH)
    pl.semaphore_wait(barrier, bands - 1)
    finish = send_ahead(
        range(1, bands - 1), bands, band, cell, own_ref, rest_ref, send_sem, recv_sem, 0
    )
    factor_steps(count, packed_ref, out_ref, work, lower, inv, diag)
    finish()


def factor_steps(count, packed_ref, out_ref, work, lower, inv, diag):
    size = count * BLK
    for i in range(count):
        row, col = place(i, 0, count)
        width = (i + 1) * BLK
        work[i * BLK : (i + 1) * BLK, :width] = packed_ref[row : row + BLK, col : col + width]
    inv[...] = jnp.zeros_like(inv)
    block = lambda i: slice(i * BLK, (i + 1) * BLK)
    diag[0] = work[:BLK, :BLK]
    invert_block(diag.at[0])
    for j in range(count):
        here, top = block(j), diag[j]
        if j + 1 < count:
            ahead = block(j + 1)
            panel = exact(work[ahead, here], top, NT)
            lower[ahead, here] = panel
            diag[j + 1] = work[ahead, ahead] - exact(panel, panel, NT)
            invert_block(diag.at[j + 1])
            for i in range(j + 2, count):
                lower[block(i), here] = exact(work[block(i), here], top, NT)
                for q in range(j + 1, i + 1):
                    work[block(i), block(q)] = work[block(i), block(q)] - exact(
                        lower[block(i), here], lower[block(q), here], NT
                    )
        if j:
            partial = exact(lower[here, : j * BLK], inv[: j * BLK, : j * BLK], NN)
            inv[here, : j * BLK] = -exact(top, partial, NN)
        inv[here, here] = top

    out_ref[...] = inv[...].astype(out_ref.dtype)


def inverse_factor(packed):
    size = packed.shape[0] * 2
    count = size // BLK
    vmem = pl.BlockSpec(memory_space=pltpu.VMEM)
    return pl.pallas_call(
        functools.partial(factor_steps, count),
        out_shape=jax.ShapeDtypeStruct((size, size), jnp.bfloat16),
        in_specs=[vmem],
        out_specs=vmem,
        scratch_shapes=[
            pltpu.VMEM((size, size), jnp.float32),
            pltpu.VMEM((size, size), jnp.float32),
            pltpu.VMEM((size, size), jnp.float32),
            pltpu.VMEM((count, BLK, BLK), jnp.float32),
        ],
    )(packed)


def inverse_and_rest(packed, own):
    bands = lax.axis_size("band")
    size = packed.shape[0] * 2
    count = size // BLK
    each = own.shape[0] // bands
    copies = (bands - 1) * (bands - 2)
    vmem = pl.BlockSpec(memory_space=pltpu.VMEM)
    return pl.pallas_call(
        functools.partial(factor_kernel, count, bands),
        out_shape=(
            jax.ShapeDtypeStruct((size, size), jnp.bfloat16),
            jax.ShapeDtypeStruct((bands - 1, bands - 2, each, BLK), own.dtype),
        ),
        in_specs=[vmem, vmem],
        out_specs=(vmem, vmem),
        scratch_shapes=[
            pltpu.VMEM((size, size), jnp.float32),
            pltpu.VMEM((size, size), jnp.float32),
            pltpu.VMEM((size, size), jnp.float32),
            pltpu.VMEM((count, BLK, BLK), jnp.float32),
            pltpu.SemaphoreType.DMA((copies,)),
            pltpu.SemaphoreType.DMA((copies,)),
        ],
        compiler_params=pltpu.CompilerParams(collective_id=1, has_side_effects=True),
    )(packed, own)


def shards(wavefunctions, stiffness, cell_scale, potential):
    if fits(*wavefunctions.shape, lax.axis_size("band"), lax.axis_size("cell")):
        slices, own, first, packed = filtered(wavefunctions, stiffness, cell_scale, potential)
        inverse, rest = inverse_and_rest(packed, own)
        return rotated_here(inverse, slices, own, first, rest)
    anchor = wavefunctions.astype(jnp.float32)
    degree_one = (
        (apply_h(wavefunctions, stiffness, cell_scale, potential) - centre * anchor) / half_width
    ).astype(jnp.bfloat16)
    one_wide = degree_one.astype(jnp.float32)
    degree_two = (
        2.0
        * (apply_h(degree_one, stiffness, cell_scale, potential) - centre * one_wide)
        / half_width
        - anchor
    ).astype(jnp.bfloat16)
    two_wide = degree_two.astype(jnp.float32)
    degree_three = (
        2.0
        * (apply_h(degree_two, stiffness, cell_scale, potential) - centre * two_wide)
        / half_width
        - one_wide
    ).astype(jnp.bfloat16)
    slices = lax.all_to_all(degree_three, "band", split_axis=1, concat_axis=0, tiled=True)
    inverse = inverse_factor(margin_packed(slices))
    rotated = jnp.dot(inverse, slices, preferred_element_type=jnp.float32).astype(jnp.bfloat16)
    return lax.all_to_all(rotated, "band", split_axis=0, concat_axis=1, tiled=True)


def solution(mesh):
    in_specs = (P("band", "cell"), P(), P("cell"), P("cell", None))
    out_specs = P("band", "cell")
    return jax.shard_map(shards, mesh=mesh, in_specs=in_specs, out_specs=out_specs, check_vma=False)
```
